32 devices in a mesh: gx: 16 (over z, y, x), gz: 2 (over core).
Axes of the slice: x: 2, y: 2, z: 4, core: 2. Of those that a mesh axis runs over, the one named last changes fastest.
Arguments:
- density: float32 [32, 64, 256], P('gx', None, 'gz'), may hold values from 0.1 to 1
- anchor_mask: int32 [32, 64, 256], P('gx', None, 'gz'), may hold values 0 or 1
- port_mask: int32 [32, 64, 256], P('gx', None, 'gz'), may hold values 0 or 1
- heater_owner: int32 [16, 2, 256, 1], P('gx', 'gz'), may hold values from 0 to 15; in each aligned block of 256 rows (0 to 255, 256 to 511, ..., all dimensions but the last counted through in order) at most 32 rows name the same one
- heater_cell: int32 [16, 2, 256], P('gx', 'gz'), may hold values from 0 to 16383
- heater_power: float32 [16, 2, 256], P('gx', 'gz'), may hold values from 1 to 10
Outputs:
- temperature: float32 [32, 64, 256], P('gx', None, 'gz')
- temperature_adjoint: float32 [32, 64, 256], P('gx', None, 'gz')
- displacement: float32 [3, 32, 64, 256], P(None, 'gx', None, 'gz')
- displacement_adjoint: float32 [3, 32, 64, 256], P(None, 'gx', None, 'gz')
- thermal_residual: float32 [2, 32, 64, 256], P(None, 'gx', None, 'gz')
- elastic_residual: float32 [2, 3, 32, 64, 256], P(None, None, 'gx', None, 'gz')
The draws below stay inside these ranges and needn't reach their ends.
Inputs may be any that keep to these rules, and one draw needn't show every extreme that they name: `heater_owner`: among the entries of one device, each block is named at most 32 times.
All inputs are finite; a program needn't handle non-finite values. No bound on the sum of `anchor_mask` or of `port_mask` on one device may be relied on, other than what follows from the above.
Results may differ from the reference program's by a relative error of at most 0.00018.
Values sent between devices are 32-bit elements; how exact they have to be, the bound alone decides.
No kernel may reach another device: no remote copies, remote signals or barrier semaphores. Data moves between devices by JAX's collectives and lax.ppermute only.
A program may use at most 64 MiB of HBM per device.

```python
import math
import jax
import jax.numpy as jnp
import numpy as np

CX = 2
CY = 64
CZ = 128
PATCHES = 256
ITERS = 2
BLOCKS_X = 16
BLOCKS_Z = 2
SLOTS = 32
NX = 32
NY = 64
NZ = 256


def touch_ends(values, key, least, high):
    longest = values.shape.index(max(values.shape))
    spots = []
    for shift in (0, 1):
        where = [jax.random.randint(jax.random.fold_in(key, axis), (), 0, length) for axis, length in enumerate(values.shape)]
        where[longest] = (where[longest] + shift) % values.shape[longest]
        spots.append(tuple(where))
    return values.at[spots[0]].set(least).at[spots[1]].set(high)


def steps_of(rng, extent, split, low, top_value):
    def one(dim, blocks):
        heights = jax.random.uniform(jax.random.fold_in(jax.random.fold_in(rng, 6), dim), (blocks,), jnp.float32, low / len(split), top_value / len(split))
        return jnp.repeat(jnp.exp(heights), extent[dim] // blocks).reshape((-1,) + (1,) * (len(extent) - dim - 1))

    level = one(*split[0])
    for cut in split[1:]:
        level = level * one(*cut)
    return level


def routed_block(stream_key, own, number, rows, number_of, top, most, skew):
    sequence = jax.random.permutation(stream_key, number_of)
    crowded, common = shares(number_of, rows * top, most, skew, True), shares(number_of, rows * top, most, skew, False)
    places = jnp.arange(number_of)

    def named(tallies, rotation):
        used = int((tallies > 0).sum())
        fixed = max(1, used // 4)
        passed = fixed + (places - fixed + rotation * (used - fixed)) % max(1, number_of - fixed)
        return jnp.zeros((number_of,), jnp.int32).at[sequence[jnp.where(places < fixed, places, passed)]].set(jnp.asarray(tallies, jnp.int32))

    tallies = jnp.where(number % 4 == 0, named(crowded, number // 4), named(common, number - number // 4 - 1))
    mixed = jax.random.permutation(jax.random.fold_in(own, 3), number_of)
    giver, sink = mixed[0:number_of // 2 * 2:2], mixed[1:number_of // 2 * 2:2]
    room = jnp.minimum(tallies[giver] - 1, most - tallies[sink]) // 2
    room = jnp.where((giver == sequence[0]) | (sink == sequence[0]) | (tallies[sink] == 0), 0, jnp.maximum(room, 0))
    passed = jax.random.randint(jax.random.fold_in(own, 4), (number_of // 2,), 0, 1 << 20) % (room + 1)
    tallies = tallies.at[giver].add(-passed).at[sink].add(passed)
    items = jnp.searchsorted(jnp.cumsum(tallies), jnp.arange(rows * top), side="right").astype(jnp.int32)
    table = items.reshape(top, rows).T
    table = table[jax.random.permutation(jax.random.fold_in(own, 1), rows)]
    rotation = jax.random.randint(jax.random.fold_in(own, 2), (rows, 1), 0, top)
    return jnp.take_along_axis(table, (jnp.arange(top)[None, :] + rotation) % top, axis=1)


def shares(amount, total, reach, skew, full):
    weights = [(1 << 20) // math.isqrt(grade ** skew) + 1 for grade in range(1, amount + 1)]
    largest = reach if full else min(reach, max(-(-total // amount), total * weights[0] // sum(weights)))
    least = 1 if total - largest >= amount - 1 else 0
    holding, rest = [largest] + [least] * (amount - 1), total - largest - least * (amount - 1)
    while rest > 0:
        movable = [i for i in range(1, amount) if holding[i] < largest] or [i for i in range(1, amount) if holding[i] < reach]
        pool, remaining = sum([weights[i] for i in movable]), rest
        for i in movable:
            more = min(reach - holding[i], max(1, remaining * weights[i] // pool), rest)
            holding[i] = holding[i] + more
            rest = rest - more
    return np.array(holding)


def setup_inputs(seed: int = 0) -> dict:
    streams_of = jax.random.split(jax.random.key(seed), 7)
    density = jnp.clip(jnp.exp(math.log(1.0) - 2.3025851 * jax.random.uniform(streams_of[0], (NX, NY, NZ), jnp.float32) ** steps_of(streams_of[0], (NX, NY, NZ), ((0, 16), (2, 2)), -0.2, 0.2)), 0.1, 1.0)
    anchor_mask = touch_ends((jax.random.randint(streams_of[1], (NX, NY, NZ), 0, 8) < 1).astype(jnp.int32), jax.random.fold_in(streams_of[1], 1), 0, 1)
    port_mask = touch_ends((jax.random.randint(streams_of[2], (NX, NY, NZ), 0, 8) < 1).astype(jnp.int32), jax.random.fold_in(streams_of[2], 1), 0, 1)
    heater_owner_keys = jax.random.split(jax.random.fold_in(streams_of[3], 1), BLOCKS_X * BLOCKS_Z * PATCHES // PATCHES)
    heater_owner_turns = jax.random.permutation(jax.random.fold_in(streams_of[3], 3), BLOCKS_X * BLOCKS_Z * PATCHES // PATCHES)
    heater_owner = jax.vmap(lambda own, number: routed_block(jax.random.fold_in(streams_of[3], 2), own, number, PATCHES, BLOCKS_X, 1, SLOTS, 2))(heater_owner_keys, heater_owner_turns).reshape((BLOCKS_X, BLOCKS_Z, PATCHES, 1))
    heater_cell = touch_ends(jax.random.randint(streams_of[4], (BLOCKS_X, BLOCKS_Z, PATCHES), 0, CX * CY * CZ), jax.random.fold_in(streams_of[4], 1), 0, (CX * CY * CZ) - 1).astype(jnp.int32)
    heater_power = jnp.clip(jnp.exp(math.log(10.0) - 2.3025851 * jax.random.uniform(streams_of[5], (BLOCKS_X, BLOCKS_Z, PATCHES), jnp.float32) ** steps_of(streams_of[5], (BLOCKS_X, BLOCKS_Z, PATCHES), ((0, 16), (1, 2)), -0.2, 0.2)), 1.0, 10.0)
    return dict(density=density, anchor_mask=anchor_mask, port_mask=port_mask, heater_owner=heater_owner, heater_cell=heater_cell, heater_power=heater_power)


KAPPA_MIN = 0.05
MODULUS_MINIMUM = 0.02
CONVECTION = 0.2
PENALTY = 10.0
JOULE_GAIN = 1.0
SIGMA_MIN = 0.1
EXPANSION = 4.0
PORT_DIRECTION = (1.0, 0.5, -0.5)


def coefficients(cubed, symmetry, floor_value):
    scalar_pairing = cubed[1:-1, 1:-1, 1:-1]
    lower_x = (floor_value + 0.5 * (scalar_pairing + cubed[:-2, 1:-1, 1:-1])) * symmetry
    upper_x = floor_value + 0.5 * (scalar_pairing + cubed[2:, 1:-1, 1:-1])
    lower_y = floor_value + 0.5 * (scalar_pairing + cubed[1:-1, :-2, 1:-1])
    upper_y = floor_value + 0.5 * (scalar_pairing + cubed[1:-1, 2:, 1:-1])
    lower_z = floor_value + 0.5 * (scalar_pairing + cubed[1:-1, 1:-1, :-2])
    upper_z = floor_value + 0.5 * (scalar_pairing + cubed[1:-1, 1:-1, 2:])
    return (lower_x, upper_x, lower_y, upper_y, lower_z, upper_z)


def stencil(padded, values, weights, diagonal_term):
    lower_x, upper_x, lower_y, upper_y, lower_z, upper_z = weights
    result = diagonal_term * values
    result = result + lower_x * (values - padded[..., :-2, 1:-1, 1:-1])
    result = result + upper_x * (values - padded[..., 2:, 1:-1, 1:-1])
    result = result + lower_y * (values - padded[..., 1:-1, :-2, 1:-1])
    result = result + upper_y * (values - padded[..., 1:-1, 2:, 1:-1])
    result = result + lower_z * (values - padded[..., 1:-1, 1:-1, :-2])
    result = result + upper_z * (values - padded[..., 1:-1, 1:-1, 2:])
    return result


def pad_last(values):
    widths = [(0, 0)] * (values.ndim - 3) + [(1, 1)] * 3
    return jnp.pad(values, widths)


def inner_products(one_side, other_side):
    return jnp.sum(one_side * other_side, axis=tuple(range(1, one_side.ndim)))


def widen(scalars):
    return scalars[:, None, None, None, None]


def reference(density, anchor_mask, port_mask, heater_owner, heater_cell, heater_power):
    cubed = pad_last(density) ** 3
    scalar_pairing = cubed[1:-1, 1:-1, 1:-1]
    symmetry = (jnp.arange(NX) > 0).astype(jnp.float32)[:, None, None]
    thermal_weights = coefficients(cubed, symmetry, KAPPA_MIN)
    elastic_weights = coefficients(cubed, symmetry, MODULUS_MINIMUM)
    owner_block = heater_owner[..., 0]
    zblock = jnp.arange(BLOCKS_Z, dtype=jnp.int32)[None, :, None]
    layer_x = heater_cell // (CY * CZ)
    layer_y = (heater_cell // CZ) % CY
    layer_z = heater_cell % CZ
    flat_index = ((owner_block * CX + layer_x) * NY + layer_y) * NZ + zblock * CZ + layer_z
    heater = jnp.zeros((NX * NY * NZ,), jnp.float32).at[flat_index.reshape(-1)].add(heater_power.reshape(-1))
    heater = heater.reshape(NX, NY, NZ)
    source = JOULE_GAIN * (SIGMA_MIN + scalar_pairing) + heater
    port_field = port_mask.astype(jnp.float32)
    joule_power_array = jnp.stack([source, port_field])
    applied = stencil(pad_last(joule_power_array), joule_power_array, thermal_weights, CONVECTION)
    correction_magnitude = inner_products(joule_power_array, joule_power_array) / inner_products(joule_power_array, applied)
    thermal_readings = correction_magnitude[:, None, None, None] * joule_power_array
    thermal_residual = joule_power_array - correction_magnitude[:, None, None, None] * applied
    mechanical_tension = (MODULUS_MINIMUM + scalar_pairing) * thermal_readings[0]
    spread = pad_last(mechanical_tension)
    spread = spread.at[0, 1:-1, 1:-1].set(mechanical_tension[0])
    thermal_force = EXPANSION * 0.5 * jnp.stack([
        spread[2:, 1:-1, 1:-1] - spread[:-2, 1:-1, 1:-1],
        spread[1:-1, 2:, 1:-1] - spread[1:-1, :-2, 1:-1],
        spread[1:-1, 1:-1, 2:] - spread[1:-1, 1:-1, :-2]])
    direction_vector = jnp.array(PORT_DIRECTION, jnp.float32)[:, None, None, None]
    elastic_rhs = jnp.stack([thermal_force, port_field[None] * direction_vector])
    anchor_term = PENALTY * anchor_mask.astype(jnp.float32)
    computed_solution = jnp.zeros_like(elastic_rhs)
    residual = elastic_rhs
    direction = elastic_rhs
    norm_now = inner_products(residual, residual)
    for iteration in range(ITERS):
        applied = stencil(pad_last(direction), direction, elastic_weights, anchor_term)
        correction_magnitude = norm_now / inner_products(direction, applied)
        computed_solution = computed_solution + widen(correction_magnitude) * direction
        residual = residual - widen(correction_magnitude) * applied
        norm_next = inner_products(residual, residual)
        direction = residual + widen(norm_next / norm_now) * direction
        norm_now = norm_next
    return thermal_readings[0], thermal_readings[1], computed_solution[0], computed_solution[1], thermal_residual, residual
```

```python
import functools

import jax
import jax.numpy as jnp
from jax import lax
from jax.experimental import pallas as pl
from jax.experimental.pallas import tpu as pltpu
from jax.sharding import PartitionSpec as P

KAPPA_MIN = 0.05
MODULUS_MINIMUM = 0.02
CONVECTION = 0.2
PENALTY = 10.0
JOULE_GAIN = 1.0
SIGMA_MIN = 0.1
EXPANSION = 4.0
PORT_DIRECTION = (1.0, 0.5, -0.5)

HALO = 3
WIDTH = 128
EDGE = 8
F32 = jnp.float32


def swap_pairs(count, offset, distance):
    pairs = []
    for low in range(offset, count - distance):
        if ((low - offset) // distance) % 2 == 0:
            pairs += [(low, low + distance), (low + distance, low)]
    return pairs


def across_z(values):
    count = lax.axis_size("gz")
    if count == 2:
        return lax.ppermute(values, "gz", [(0, 1), (1, 0)])
    upper = lax.ppermute(values, "gz", [(i + 1, i) for i in range(count - 1)])
    lower = lax.ppermute(values, "gz", [(i, i + 1) for i in range(count - 1)])
    lanes = lax.broadcasted_iota(jnp.int32, values.shape, values.ndim - 1)
    return jnp.where(lanes < WIDTH // 2, upper, lower)


def heater_kernel(entries_ref, heat_ref, rows_ref, lanes_ref, total_ref, *, layers, height, block):
    sources = entries_ref.shape[0]
    entries = entries_ref.shape[2]
    slabs = layers + 2 * HALO
    base = lax.axis_index("gx") * layers - HALO
    row_ids = lax.broadcasted_iota(jnp.int32, (slabs * height, entries), 0)
    lane_ids = lax.broadcasted_iota(jnp.int32, (WIDTH, entries), 0)
    plane = height * WIDTH

    def one_block(start):
        for k in range(block):
            table = entries_ref[start + k]
            owner = table[0:1].astype(jnp.int32)
            cell = table[1:2].astype(jnp.int32)
            power = table[2:3]
            rest = cell % plane
            row = (owner * layers + cell // plane - base) * height + rest // WIDTH
            lane = rest % WIDTH
            high = power.astype(jnp.bfloat16).astype(F32)
            low = power - high
            here = slice(k * entries, (k + 1) * entries)
            rows_ref[:, here] = jnp.where(row_ids == row, 1.0, 0.0).astype(jnp.bfloat16)
            match = lane_ids == lane
            lanes_ref[0:WIDTH, here] = jnp.where(match, high, 0.0).astype(jnp.bfloat16)
            lanes_ref[WIDTH:, here] = jnp.where(match, low, 0.0).astype(jnp.bfloat16)
        return lax.dot_general(
            rows_ref[...], lanes_ref[...], (((1,), (1,)), ((), ())), preferred_element_type=F32
        )

    total = one_block(0)
    if sources > block:
        total_ref[...] = total

        @pl.loop(1, sources // block)
        def _(step):
            total_ref[...] += one_block(step * block)

        total = total_ref[...]
    heat = total[:, :WIDTH] + total[:, WIDTH:]
    heat_ref[...] = heat.reshape(heat_ref.shape)


def scatter_heat(entries, layers, height):
    sources, _, count = entries.shape
    block = min(sources, 16)
    slabs = layers + 2 * HALO
    return pl.pallas_call(
        functools.partial(heater_kernel, layers=layers, height=height, block=block),
        out_shape=jax.ShapeDtypeStruct((slabs, height, WIDTH), F32),
        in_specs=[pl.BlockSpec(memory_space=pltpu.VMEM)],
        out_specs=pl.BlockSpec(memory_space=pltpu.VMEM),
        scratch_shapes=[
            pltpu.VMEM((slabs * height, block * count), jnp.bfloat16),
            pltpu.VMEM((2 * WIDTH, block * count), jnp.bfloat16),
            pltpu.VMEM((slabs * height, 2 * WIDTH), F32),
        ],
        name="heater_scatter",
    )(entries)


def main_kernel(
    density_ref, anchor_ref, port_ref, own_z_ref, first_ref, first_z_ref, second_ref, second_z_ref,
    far_ref, far_z_ref, heat_ref, heat_z_ref,
    source_ref, applied_ref, force_ref, image_ref, image2_ref, pimage_ref, pimage2_ref, sums_ref,
    cub, stress, src, prt, force, image,
):
    height = density_ref.shape[1]
    gx = lax.axis_index("gx")
    gz = lax.axis_index("gz")
    last_x = lax.axis_size("gx") - 1
    last_z = lax.axis_size("gz") - 1
    even = gx % 2 == 0
    low_pair = gx % 4 < 2

    def flag(condition):
        return jnp.where(condition, 1.0, 0.0).astype(F32)

    tile = (height, WIDTH)
    lanes = lax.broadcasted_iota(jnp.int32, tile, 1)
    is_last = lanes == WIDTH - 1
    is_first = lanes == 0
    z_valid = jnp.where(lanes < WIDTH // 2, flag(gz < last_z), flag(gz > 0))
    x_valid = [
        flag(gx >= 2), flag(gx >= 1), flag(gx >= 1), None, None,
        flag(gx < last_x), flag(gx < last_x), flag(gx < last_x - 1),
    ]
    symmetry = flag(gx > 0)

    def masked(side, layer, value):
        if side:
            value = value * z_valid
        if x_valid[layer] is not None:
            value = value * x_valid[layer]
        return value

    def load(ref, side, layer, shift=0):
        return ref[side, layer, EDGE + shift : EDGE + shift + height, :]

    def store(ref, side, layer, value):
        ref[side, layer, EDGE : EDGE + height, :] = value

    def z_up(pair):
        a, b = (pltpu.roll(v, WIDTH - 1, 1) for v in pair)
        return jnp.where(is_last, b, a), jnp.where(is_last, a, b)

    def z_down(pair):
        a, b = (pltpu.roll(v, 1, 1) for v in pair)
        return jnp.where(is_first, b, a), jnp.where(is_first, a, b)

    edge_rows = jnp.zeros((EDGE, WIDTH), F32)
    for ref in (cub, stress, src, prt, force, image):
        for side in range(2):
            for layer in range(ref.shape[1]):
                ref[side, layer, 0:EDGE, :] = edge_rows
                ref[side, layer, EDGE + height :, :] = edge_rows

    def lower(side, k):
        a, b = (first_z_ref, second_z_ref) if side else (first_ref, second_ref)
        return jnp.where(even, b[k], a[k])

    def upper(side, k):
        a, b = (first_z_ref, second_z_ref) if side else (first_ref, second_ref)
        return jnp.where(even, a[k], b[k])

    def far(side, low):
        ref = far_z_ref if side else far_ref
        return jnp.where(low_pair, ref[1], ref[0]) if low else jnp.where(low_pair, ref[0], ref[1])

    def density_of(side, layer):
        if layer == 0:
            return far(side, True)
        if layer == 7:
            return far(side, False)
        if layer in (1, 2):
            return lower(side, layer - 1)
        if layer in (5, 6):
            return upper(side, layer - 5)
        return own_z_ref[layer - 3] if side else density_ref[layer - 3]

    def port_of(side, layer):
        if layer in (1, 2):
            return lower(side, layer + 1)
        if layer in (5, 6):
            return upper(side, layer - 3)
        return own_z_ref[layer - 1] if side else port_ref[layer - 3].astype(F32)

    def anchor_of(side, layer):
        if layer == 2:
            return lower(side, 4)
        if layer == 5:
            return upper(side, 4)
        return own_z_ref[layer + 1] if side else anchor_ref[layer - 3].astype(F32)

    for layer in range(8):
        for side in range(2):
            d = masked(side, layer, density_of(side, layer))
            c = d * d * d
            heat = (heat_z_ref if side else heat_ref)[layer]
            s = masked(side, layer, JOULE_GAIN * (SIGMA_MIN + c) + heat)
            store(cub, side, layer, c)
            store(stress, side, layer, (MODULUS_MINIMUM + c) * s)
            if 2 <= layer <= 5:
                store(src, side, layer - 2, s)
            if side == 0 and layer in (3, 4):
                source_ref[layer - 3] = s
            if 1 <= layer <= 6:
                store(prt, side, layer - 1, masked(side, layer, port_of(side, layer)))
    for side in range(2):
        for layer, block in ((0, 1), (2, 0)):
            mirrored = jnp.where(gx == block, load(stress, side, layer + 1), load(stress, side, layer))
            store(stress, side, layer, mirrored)

    half = EXPANSION * 0.5
    for layer in range(1, 7):
        pair = [load(stress, side, layer) for side in range(2)]
        up, down = z_up(pair), z_down(pair)
        for side in range(2):
            parts = (
                load(stress, side, layer + 1) - load(stress, side, layer - 1),
                load(stress, side, layer, 1) - load(stress, side, layer, -1),
                up[side] - down[side],
            )
            for k in range(3):
                value = masked(side, layer, half * parts[k])
                store(force, side, k * 6 + layer - 1, value)
                if side == 0 and layer in (3, 4):
                    force_ref[k, layer - 3] = value

    def face(a, b):
        return MODULUS_MINIMUM + 0.5 * (a + b)

    sums = {}

    def accumulate(name, value):
        value = jnp.sum(value.reshape(height // 8, 8, WIDTH), axis=0)
        sums[name] = value if name not in sums else sums[name] + value

    def weights_of(layer):
        pair = [load(cub, side, layer) for side in range(2)]
        up, down = z_up(pair), z_down(pair)
        result = []
        for side in range(2):
            c = pair[side]
            x_low = face(load(cub, side, layer - 1), c)
            if layer == 3:
                x_low = x_low * symmetry
            result.append(
                (
                    x_low,
                    face(load(cub, side, layer + 1), c),
                    face(load(cub, side, layer, -1), c),
                    face(load(cub, side, layer, 1), c),
                    face(down[side], c),
                    face(up[side], c),
                )
            )
        return result

    def differences(ref, index, sides):
        pair = [load(ref, side, index) for side in range(2)]
        up, down = z_up(pair), z_down(pair)
        result = []
        for side in sides:
            v = pair[side]
            result.append(
                (
                    v,
                    (
                        v - load(ref, side, index - 1),
                        v - load(ref, side, index + 1),
                        v - load(ref, side, index, -1),
                        v - load(ref, side, index, 1),
                        v - down[side],
                        v - up[side],
                    ),
                )
            )
        return result

    def weighted(weights, parts):
        total = weights[0] * parts[0]
        for w, p in zip(weights[1:], parts[1:]):
            total = total + w * p
        return total

    own_weights, own_anchor = {}, {}
    spread = KAPPA_MIN - MODULUS_MINIMUM
    for layer in range(2, 6):
        weights = weights_of(layer)
        anchors = [PENALTY * anchor_of(side, layer) for side in range(2)]
        own = layer in (3, 4)
        if own:
            own_weights[layer], own_anchor[layer] = weights[0], anchors[0]
        for k in range(4):
            ref, index = (force, k * 6 + layer - 1) if k < 3 else (prt, layer - 1)
            for side, (v, parts) in enumerate(differences(ref, index, range(2))):
                flux = weighted(weights[side], parts)
                value = masked(side, layer, flux + anchors[side] * v)
                store(image, side, k * 4 + layer - 2, value)
                if own and side == 0:
                    if k < 3:
                        image_ref[k, layer - 3] = value
                        accumulate("n0", v * v)
                        accumulate("m0", v * value)
                    else:
                        pimage_ref[layer - 3] = value
                        accumulate("n1", v * v)
                        accumulate("m1", v * value)
                        first = parts[0] * symmetry if layer == 3 else parts[0]
                        plain = first + parts[1] + parts[2] + parts[3] + parts[4] + parts[5]
                        heat_image = flux + spread * plain + CONVECTION * v
                        applied_ref[1, layer - 3] = heat_image
                        accumulate("k1", v * heat_image)
        if own:
            v, parts = differences(src, layer - 2, (0,))[0]
            heat_weights = [w + spread for w in weights[0]]
            if layer == 3:
                heat_weights[0] = weights[0][0] + spread * symmetry
            heat_image = weighted(heat_weights, parts) + CONVECTION * v
            applied_ref[0, layer - 3] = heat_image
            accumulate("k", v * heat_image)
            accumulate("q", v * v)

    def total(value):
        return jnp.sum(jnp.sum(value, axis=0, keepdims=True), axis=1, keepdims=True)

    final = {name: total(sums[name]) for name in ("n0", "m0", "n1", "m1", "k", "q", "k1")}
    shift = []
    for member in range(2):
        n, m = final["n%d" % member], final["m%d" % member]
        shift.append(jnp.where(n > 0.0, m / jnp.where(n > 0.0, n, 1.0), 0.0))
    for layer in (3, 4):
        for k in range(4):
            v, parts = differences(image, k * 4 + layer - 2, (0,))[0]
            value = weighted(own_weights[layer], parts) + own_anchor[layer] * v
            if k < 3:
                image2_ref[k, layer - 3] = value
                start = load(force, 0, k * 6 + layer - 1)
            else:
                pimage2_ref[layer - 3] = value
                start = load(prt, 0, layer - 1)
            theta = shift[k // 3]
            r = v - theta * start
            y = value - theta * v
            accumulate("s%d" % (k // 3), r * r)
            accumulate("t%d" % (k // 3), r * y)
            accumulate("c%d" % (k // 3), start * y)
    for member in range(2):
        for name in "stc":
            final[name + str(member)] = total(sums[name + str(member)])
    columns = (
        final["q"], final["k"], final["n1"], final["k1"],
        final["n0"], final["m0"], final["s0"], final["t0"], final["c0"] + final["s0"],
        final["n1"], final["m1"], final["s1"], final["t1"], final["c1"] + final["s1"],
    )
    lane = lax.broadcasted_iota(jnp.int32, (1, WIDTH), 1)
    row = jnp.zeros((1, WIDTH), F32)
    for k, column in enumerate(columns):
        row = jnp.where(lane == k, column, row)
    sums_ref[...] = jnp.broadcast_to(row[None], sums_ref.shape)


def main_stage(arguments, devices, layers, height):
    own = (layers, height, WIDTH)
    vectors = (3,) + own
    shapes = [own, (2,) + own, vectors, vectors, vectors, own, own, (devices, 1, WIDTH)]

    def field(count):
        return pltpu.VMEM((2, count, height + 2 * EDGE, WIDTH), F32)

    vmem = pl.BlockSpec(memory_space=pltpu.VMEM)
    return pl.pallas_call(
        main_kernel,
        out_shape=[jax.ShapeDtypeStruct(s, F32) for s in shapes],
        in_specs=[vmem] * len(arguments),
        out_specs=[vmem] * len(shapes),
        scratch_shapes=[field(8), field(8), field(4), field(6), field(18), field(16)],
        name="operators",
    )(*arguments)


def final_kernel(
    table_ref, source_ref, port_ref, applied_ref, force_ref, image_ref, image2_ref, pimage_ref, pimage2_ref,
    temperature_ref, adjoint_ref, displacement_ref, displacement_adjoint_ref, thermal_ref, elastic_ref,
):
    table = table_ref[...].reshape(table_ref.shape[0], WIDTH)

    def column(k):
        return table[:, k : k + 1]

    def total(value):
        return jnp.sum(value, axis=0, keepdims=True)

    step0 = total(column(0)) / total(column(1))
    step1 = total(column(2)) / total(column(3))

    def solve(first):
        n_all, m_all = column(first), column(first + 1)
        n, m = total(n_all), total(m_all)
        theta = m / n
        local = jnp.where(n_all > 0.0, m_all / jnp.where(n_all > 0.0, n_all, 1.0), 0.0)
        gap = local - theta
        s = total(column(first + 2) + gap * gap * n_all)
        t = total(column(first + 3) + gap * column(first + 4) + gap * gap * m_all)
        alpha0 = n / m
        beta = s * alpha0 * alpha0 / n
        alpha1 = s / (t - s * s / m)
        return alpha0, beta, alpha1

    def outcome(coefficients, b, w, u):
        alpha0, beta, alpha1 = coefficients
        r = b - alpha0 * w
        x = alpha0 * b + alpha1 * (r + beta * b)
        r = r - alpha1 * ((w - alpha0 * u) + beta * w)
        return x, r

    forward, adjoint = solve(4), solve(9)
    for layer in range(source_ref.shape[0]):
        source = source_ref[layer]
        port = port_ref[layer].astype(F32)
        temperature_ref[layer] = step0 * source
        adjoint_ref[layer] = step1 * port
        thermal_ref[0, layer] = source - step0 * applied_ref[0, layer]
        thermal_ref[1, layer] = port - step1 * applied_ref[1, layer]
        for k in range(3):
            x, r = outcome(forward, force_ref[k, layer], image_ref[k, layer], image2_ref[k, layer])
            displacement_ref[k, layer] = step0 * x
            elastic_ref[0, k, layer] = step0 * r
        x, r = outcome(adjoint, port, pimage_ref[layer], pimage2_ref[layer])
        for k in range(3):
            displacement_adjoint_ref[k, layer] = PORT_DIRECTION[k] * x
            elastic_ref[1, k, layer] = PORT_DIRECTION[k] * r


def final_stage(arguments, layers, height):
    own = (layers, height, WIDTH)
    shapes = [own, own, (3,) + own, (3,) + own, (2,) + own, (2, 3) + own]
    vmem = pl.BlockSpec(memory_space=pltpu.VMEM)
    return pl.pallas_call(
        final_kernel,
        out_shape=[jax.ShapeDtypeStruct(s, F32) for s in shapes],
        in_specs=[vmem] * len(arguments),
        out_specs=[vmem] * len(shapes),
        name="outputs",
    )(*arguments)


def per_device(density, anchor_mask, port_mask, heater_owner, heater_cell, heater_power):
    layers, height, _ = density.shape
    count = lax.axis_size("gx")
    devices = count * lax.axis_size("gz")
    gx = lax.axis_index("gx")
    entries = jnp.stack(
        [heater_owner.reshape(-1).astype(F32), heater_cell.reshape(-1).astype(F32), heater_power.reshape(-1)]
    )
    entries = lax.all_to_all(
        jnp.broadcast_to(entries[None], (count,) + entries.shape), "gx", 0, 0, tiled=True
    )
    port = port_mask.astype(F32)
    anchor = anchor_mask.astype(F32)
    even = gx % 2 == 0
    low_pair = gx % 4 < 2
    core = jnp.concatenate([density, port])
    first = jnp.concatenate([core, jnp.where(even, anchor[1:2], anchor[0:1])])
    second = jnp.concatenate([core, jnp.where(even, anchor[0:1], anchor[1:2])])
    far_one = jnp.where(low_pair, density[1:2], density[0:1])
    far_two = jnp.where(low_pair, density[0:1], density[1:2])
    first = lax.ppermute(first, "gx", swap_pairs(count, 0, 1))
    second = lax.ppermute(second, "gx", swap_pairs(count, 1, 1))
    far_one = lax.ppermute(far_one, "gx", swap_pairs(count, 0, 2))
    far_two = lax.ppermute(far_two, "gx", swap_pairs(count, 2, 2))
    far = jnp.concatenate([far_one, far_two])
    own_z = across_z(jnp.concatenate([core, anchor]))
    first_z = across_z(first)
    second_z = across_z(second)
    far_z = across_z(far)
    heat = scatter_heat(entries, layers, height)
    heat_z = across_z(heat)
    source, applied, force, image, image2, pimage, pimage2, sums = main_stage(
        (density, anchor_mask, port_mask, own_z, first, first_z, second, second_z, far, far_z, heat, heat_z),
        devices, layers, height,
    )
    table = lax.all_to_all(sums, ("gx", "gz"), 0, 0, tiled=True)
    return tuple(
        final_stage(
            (table, source, port_mask, applied, force, image, image2, pimage, pimage2), layers, height
        )
    )


def solution(mesh):
    in_specs = (
        P("gx", None, "gz"),
        P("gx", None, "gz"),
        P("gx", None, "gz"),
        P("gx", "gz", None, None),
        P("gx", "gz", None),
        P("gx", "gz", None),
    )
    out_specs = (
        P("gx", None, "gz"),
        P("gx", None, "gz"),
        P(None, "gx", None, "gz"),
        P(None, "gx", None, "gz"),
        P(None, "gx", None, "gz"),
        P(None, None, "gx", None, "gz"),
    )
    return jax.shard_map(
        per_device, mesh=mesh, in_specs=in_specs, out_specs=out_specs, check_vma=False
    )
```

```python
import functools

import jax
import jax.numpy as jnp
from jax import lax
from jax.experimental import pallas as pl
from jax.experimental.pallas import tpu as pltpu
from jax.sharding import PartitionSpec as P


KAPPA_MIN = 0.05
MODULUS_MINIMUM = 0.02
CONVECTION = 0.2
PENALTY = 10.0
JOULE_GAIN = 1.0
SIGMA_MIN = 0.1
EXPANSION = 4.0
PORT_DIRECTION = (1.0, 0.5, -0.5)

HALO = 3
WIDTH = 128
EDGE = 8
VMEM_LIMIT = 16 << 20
F32 = jnp.float32


def swap_pairs(count, offset, distance):
    pairs = []
    for low in range(offset, count - distance):
        if ((low - offset) // distance) % 2 == 0:
            pairs += [(low, low + distance), (low + distance, low)]
    return pairs


def across_z(values):
    count = lax.axis_size("gz")
    if count == 2:
        return lax.ppermute(values, "gz", [(0, 1), (1, 0)])
    upper = lax.ppermute(values, "gz", [(i + 1, i) for i in range(count - 1)])
    lower = lax.ppermute(values, "gz", [(i, i + 1) for i in range(count - 1)])
    lanes = lax.broadcasted_iota(jnp.int32, values.shape, values.ndim - 1)
    return jnp.where(lanes < WIDTH // 2, upper, lower)


def prepare_kernel(
    density_hbm, anchor_hbm, port_hbm, owner_hbm, cell_hbm, power_hbm,
    first_ref, second_ref, far_one_ref, far_two_ref, own_ref, entries_ref,
    density_ref, anchor_ref, port_ref, owner_ref, cell_ref, power_ref, arrived,
):
    layers = density_ref.shape[0]
    sources = (owner_hbm, cell_hbm, power_hbm, density_hbm, port_hbm, anchor_hbm)
    targets = (owner_ref, cell_ref, power_ref, density_ref, port_ref, anchor_ref)
    copies = [
        pltpu.make_async_copy(source, target, arrived.at[k])
        for k, (source, target) in enumerate(zip(sources, targets))
    ]
    for copy in copies:
        copy.start()
    gx = lax.axis_index("gx")
    even = gx % 2 == 0
    low_pair = gx % 4 < 2
    for copy in copies[:3]:
        copy.wait()
    owner = owner_ref[...].astype(F32)
    cell = cell_ref[...].astype(F32)
    power = power_ref[...]
    for k in range(entries_ref.shape[0]):
        entries_ref[k, 0:1] = owner
        entries_ref[k, 1:2] = cell
        entries_ref[k, 2:3] = power
    copies[3].wait()
    for layer in range(layers):
        density = density_ref[layer]
        for ref in (first_ref, second_ref, own_ref):
            ref[layer] = density
    below, above = density_ref[0], density_ref[layers - 1]
    far_one_ref[0] = jnp.where(low_pair, above, below)
    far_two_ref[0] = jnp.where(low_pair, below, above)
    copies[4].wait()
    for layer in range(layers):
        port = port_ref[layer].astype(F32)
        for ref in (first_ref, second_ref, own_ref):
            ref[layers + layer] = port
    copies[5].wait()
    for layer in range(layers):
        own_ref[2 * layers + layer] = anchor_ref[layer].astype(F32)
    below, above = anchor_ref[0].astype(F32), anchor_ref[layers - 1].astype(F32)
    first_ref[2 * layers] = jnp.where(even, above, below)
    second_ref[2 * layers] = jnp.where(even, below, above)


def prepare(arguments, sources):
    layers, height, _ = arguments[0].shape
    plane = (height, WIDTH)
    shapes = [
        (2 * layers + 1,) + plane, (2 * layers + 1,) + plane, (1,) + plane, (1,) + plane,
        (3 * layers,) + plane, (sources, 3, arguments[-1].shape[1]),
    ]
    return pl.pallas_call(
        prepare_kernel,
        out_shape=[jax.ShapeDtypeStruct(s, F32) for s in shapes],
        in_specs=[pl.BlockSpec(memory_space=pltpu.HBM)] * len(arguments),
        out_specs=[pl.BlockSpec(memory_space=pltpu.VMEM)] * len(shapes),
        scratch_shapes=[pltpu.VMEM(a.shape, a.dtype) for a in arguments]
        + [pltpu.SemaphoreType.DMA((len(arguments),))],
        compiler_params=pltpu.CompilerParams(vmem_limit_bytes=VMEM_LIMIT),
        name="prepare",
    )(*arguments)


def heater_kernel(entries_ref, heat_ref, rows_ref, lanes_ref, total_ref, *, layers, height, block):
    sources = entries_ref.shape[0]
    entries = entries_ref.shape[2]
    slabs = layers + 2 * HALO
    base = lax.axis_index("gx") * layers - HALO
    row_ids = lax.broadcasted_iota(jnp.int32, (slabs * height, entries), 0)
    lane_ids = lax.broadcasted_iota(jnp.int32, (WIDTH, entries), 0)
    plane = height * WIDTH

    def one_block(start):
        for k in range(block):
            table = entries_ref[start + k]
            owner = table[0:1].astype(jnp.int32)
            cell = table[1:2].astype(jnp.int32)
            power = table[2:3]
            rest = cell % plane
            row = (owner * layers + cell // plane - base) * height + rest // WIDTH
            lane = rest % WIDTH
            high = power.astype(jnp.bfloat16).astype(F32)
            low = power - high
            here = slice(k * entries, (k + 1) * entries)
            rows_ref[:, here] = jnp.where(row_ids == row, 1.0, 0.0).astype(jnp.bfloat16)
            match = lane_ids == lane
            lanes_ref[0:WIDTH, here] = jnp.where(match, high, 0.0).astype(jnp.bfloat16)
            lanes_ref[WIDTH:, here] = jnp.where(match, low, 0.0).astype(jnp.bfloat16)
        return lax.dot_general(
            rows_ref[...], lanes_ref[...], (((1,), (1,)), ((), ())), preferred_element_type=F32
        )

    total = one_block(0)
    if sources > block:
        total_ref[...] = total

        @pl.loop(1, sources // block)
        def _(step):
            total_ref[...] += one_block(step * block)

        total = total_ref[...]
    heat = total[:, :WIDTH] + total[:, WIDTH:]
    heat_ref[...] = heat.reshape(heat_ref.shape)


def scatter_heat(entries, layers, height):
    sources, _, count = entries.shape
    block = min(sources, 16)
    slabs = layers + 2 * HALO
    return pl.pallas_call(
        functools.partial(heater_kernel, layers=layers, height=height, block=block),
        out_shape=jax.ShapeDtypeStruct((slabs, height, WIDTH), F32),
        in_specs=[pl.BlockSpec(memory_space=pltpu.VMEM)],
        out_specs=pl.BlockSpec(memory_space=pltpu.VMEM),
        scratch_shapes=[
            pltpu.VMEM((slabs * height, block * count), jnp.bfloat16),
            pltpu.VMEM((2 * WIDTH, block * count), jnp.bfloat16),
            pltpu.VMEM((slabs * height, 2 * WIDTH), F32),
        ],
        compiler_params=pltpu.CompilerParams(vmem_limit_bytes=VMEM_LIMIT),
        name="heater_scatter",
    )(entries)


def main_kernel(
    own_ref, own_z_ref, first_ref, first_z_ref, second_ref, second_z_ref,
    far_ref, far_z_ref, heat_ref, heat_z_ref,
    source_ref, applied_ref, force_ref, image_ref, image2_ref, pimage_ref, pimage2_ref, sums_ref,
    cub, stress, src, prt, force, image,
):
    height = own_ref.shape[1]
    gx = lax.axis_index("gx")
    gz = lax.axis_index("gz")
    last_x = lax.axis_size("gx") - 1
    last_z = lax.axis_size("gz") - 1
    even = gx % 2 == 0
    low_pair = gx % 4 < 2

    def flag(condition):
        return jnp.where(condition, 1.0, 0.0).astype(F32)

    tile = (height, WIDTH)
    lanes = lax.broadcasted_iota(jnp.int32, tile, 1)
    is_last = lanes == WIDTH - 1
    is_first = lanes == 0
    z_valid = jnp.where(lanes < WIDTH // 2, flag(gz < last_z), flag(gz > 0))
    x_valid = [
        flag(gx >= 2), flag(gx >= 1), flag(gx >= 1), None, None,
        flag(gx < last_x), flag(gx < last_x), flag(gx < last_x - 1),
    ]
    symmetry = flag(gx > 0)

    def masked(side, layer, value):
        if side:
            value = value * z_valid
        if x_valid[layer] is not None:
            value = value * x_valid[layer]
        return value

    def load(ref, side, layer, shift=0):
        return ref[side, layer, EDGE + shift : EDGE + shift + height, :]

    def store(ref, side, layer, value):
        ref[side, layer, EDGE : EDGE + height, :] = value

    def z_up(pair):
        a, b = (pltpu.roll(v, WIDTH - 1, 1) for v in pair)
        return jnp.where(is_last, b, a), jnp.where(is_last, a, b)

    def z_down(pair):
        a, b = (pltpu.roll(v, 1, 1) for v in pair)
        return jnp.where(is_first, b, a), jnp.where(is_first, a, b)

    edge_rows = jnp.zeros((EDGE, WIDTH), F32)
    for ref in (cub, stress, src, prt, force, image):
        for side in range(2):
            for layer in range(ref.shape[1]):
                ref[side, layer, 0:EDGE, :] = edge_rows
                ref[side, layer, EDGE + height :, :] = edge_rows

    def lower(side, k):
        a, b = (first_z_ref, second_z_ref) if side else (first_ref, second_ref)
        return jnp.where(even, b[k], a[k])

    def upper(side, k):
        a, b = (first_z_ref, second_z_ref) if side else (first_ref, second_ref)
        return jnp.where(even, a[k], b[k])

    def far(side, low):
        ref = far_z_ref if side else far_ref
        return jnp.where(low_pair, ref[1], ref[0]) if low else jnp.where(low_pair, ref[0], ref[1])

    def density_of(side, layer):
        if layer == 0:
            return far(side, True)
        if layer == 7:
            return far(side, False)
        if layer in (1, 2):
            return lower(side, layer - 1)
        if layer in (5, 6):
            return upper(side, layer - 5)
        return (own_z_ref if side else own_ref)[layer - 3]

    def port_of(side, layer):
        if layer in (1, 2):
            return lower(side, layer + 1)
        if layer in (5, 6):
            return upper(side, layer - 3)
        return (own_z_ref if side else own_ref)[layer - 1]

    def anchor_of(side, layer):
        if layer == 2:
            return lower(side, 4)
        if layer == 5:
            return upper(side, 4)
        return (own_z_ref if side else own_ref)[layer + 1]

    for layer in range(8):
        for side in range(2):
            d = masked(side, layer, density_of(side, layer))
            c = d * d * d
            heat = (heat_z_ref if side else heat_ref)[layer]
            s = masked(side, layer, JOULE_GAIN * (SIGMA_MIN + c) + heat)
            store(cub, side, layer, c)
            store(stress, side, layer, (MODULUS_MINIMUM + c) * s)
            if 2 <= layer <= 5:
                store(src, side, layer - 2, s)
            if side == 0 and layer in (3, 4):
                source_ref[layer - 3] = s
            if 1 <= layer <= 6:
                store(prt, side, layer - 1, masked(side, layer, port_of(side, layer)))
    for side in range(2):
        for layer, block in ((0, 1), (2, 0)):
            mirrored = jnp.where(gx == block, load(stress, side, layer + 1), load(stress, side, layer))
            store(stress, side, layer, mirrored)

    half = EXPANSION * 0.5
    for layer in range(1, 7):
        pair = [load(stress, side, layer) for side in range(2)]
        up, down = z_up(pair), z_down(pair)
        for side in range(2):
            parts = (
                load(stress, side, layer + 1) - load(stress, side, layer - 1),
                load(stress, side, layer, 1) - load(stress, side, layer, -1),
                up[side] - down[side],
            )
            for k in range(3):
                value = masked(side, layer, half * parts[k])
                store(force, side, k * 6 + layer - 1, value)
                if side == 0 and layer in (3, 4):
                    force_ref[k, layer - 3] = value

    def face(a, b):
        return MODULUS_MINIMUM + 0.5 * (a + b)

    sums = {}

    def accumulate(name, value):
        value = jnp.sum(value.reshape(height // 8, 8, WIDTH), axis=0)
        sums[name] = value if name not in sums else sums[name] + value

    def weights_of(layer):
        pair = [load(cub, side, layer) for side in range(2)]
        up, down = z_up(pair), z_down(pair)
        result = []
        for side in range(2):
            c = pair[side]
            x_low = face(load(cub, side, layer - 1), c)
            if layer == 3:
                x_low = x_low * symmetry
            result.append(
                (
                    x_low,
                    face(load(cub, side, layer + 1), c),
                    face(load(cub, side, layer, -1), c),
                    face(load(cub, side, layer, 1), c),
                    face(down[side], c),
                    face(up[side], c),
                )
            )
        return result

    def differences(ref, index, sides):
        pair = [load(ref, side, index) for side in range(2)]
        up, down = z_up(pair), z_down(pair)
        result = []
        for side in sides:
            v = pair[side]
            result.append(
                (
                    v,
                    (
                        v - load(ref, side, index - 1),
                        v - load(ref, side, index + 1),
                        v - load(ref, side, index, -1),
                        v - load(ref, side, index, 1),
                        v - down[side],
                        v - up[side],
                    ),
                )
            )
        return result

    def weighted(weights, parts):
        total = weights[0] * parts[0]
        for w, p in zip(weights[1:], parts[1:]):
            total = total + w * p
        return total

    own_weights, own_anchor = {}, {}
    spread = KAPPA_MIN - MODULUS_MINIMUM
    for layer in range(2, 6):
        weights = weights_of(layer)
        anchors = [PENALTY * anchor_of(side, layer) for side in range(2)]
        own = layer in (3, 4)
        if own:
            own_weights[layer], own_anchor[layer] = weights[0], anchors[0]
        for k in range(4):
            ref, index = (force, k * 6 + layer - 1) if k < 3 else (prt, layer - 1)
            for side, (v, parts) in enumerate(differences(ref, index, range(2))):
                flux = weighted(weights[side], parts)
                value = masked(side, layer, flux + anchors[side] * v)
                store(image, side, k * 4 + layer - 2, value)
                if own and side == 0:
                    if k < 3:
                        image_ref[k, layer - 3] = value
                        accumulate("n0", v * v)
                        accumulate("m0", v * value)
                    else:
                        pimage_ref[layer - 3] = value
                        accumulate("n1", v * v)
                        accumulate("m1", v * value)
                        first = parts[0] * symmetry if layer == 3 else parts[0]
                        plain = first + parts[1] + parts[2] + parts[3] + parts[4] + parts[5]
                        heat_image = flux + spread * plain + CONVECTION * v
                        applied_ref[1, layer - 3] = heat_image
                        accumulate("k1", v * heat_image)
        if own:
            v, parts = differences(src, layer - 2, (0,))[0]
            heat_weights = [w + spread for w in weights[0]]
            if layer == 3:
                heat_weights[0] = weights[0][0] + spread * symmetry
            heat_image = weighted(heat_weights, parts) + CONVECTION * v
            applied_ref[0, layer - 3] = heat_image
            accumulate("k", v * heat_image)
            accumulate("q", v * v)

    def total(value):
        return jnp.sum(jnp.sum(value, axis=0, keepdims=True), axis=1, keepdims=True)

    final = {name: total(sums[name]) for name in ("n0", "m0", "n1", "m1", "k", "q", "k1")}
    shift = []
    for member in range(2):
        n, m = final["n%d" % member], final["m%d" % member]
        shift.append(jnp.where(n > 0.0, m / jnp.where(n > 0.0, n, 1.0), 0.0))
    for layer in (3, 4):
        for k in range(4):
            v, parts = differences(image, k * 4 + layer - 2, (0,))[0]
            value = weighted(own_weights[layer], parts) + own_anchor[layer] * v
            if k < 3:
                image2_ref[k, layer - 3] = value
                start = load(force, 0, k * 6 + layer - 1)
            else:
                pimage2_ref[layer - 3] = value
                start = load(prt, 0, layer - 1)
            theta = shift[k // 3]
            r = v - theta * start
            y = value - theta * v
            accumulate("s%d" % (k // 3), r * r)
            accumulate("t%d" % (k // 3), r * y)
            accumulate("c%d" % (k // 3), start * y)
    for member in range(2):
        for name in "stc":
            final[name + str(member)] = total(sums[name + str(member)])
    columns = (
        final["q"], final["k"], final["n1"], final["k1"],
        final["n0"], final["m0"], final["s0"], final["t0"], final["c0"] + final["s0"],
        final["n1"], final["m1"], final["s1"], final["t1"], final["c1"] + final["s1"],
    )
    lane = lax.broadcasted_iota(jnp.int32, (1, WIDTH), 1)
    row = jnp.zeros((1, WIDTH), F32)
    for k, column in enumerate(columns):
        row = jnp.where(lane == k, column, row)
    sums_ref[...] = jnp.broadcast_to(row[None], sums_ref.shape)


def main_stage(arguments, devices, layers, height):
    own = (layers, height, WIDTH)
    vectors = (3,) + own
    shapes = [own, (2,) + own, vectors, vectors, vectors, own, own, (devices, 1, WIDTH)]

    def field(count):
        return pltpu.VMEM((2, count, height + 2 * EDGE, WIDTH), F32)

    vmem = pl.BlockSpec(memory_space=pltpu.VMEM)
    return pl.pallas_call(
        main_kernel,
        out_shape=[jax.ShapeDtypeStruct(s, F32) for s in shapes],
        in_specs=[vmem] * len(arguments),
        out_specs=[vmem] * len(shapes),
        scratch_shapes=[field(8), field(8), field(4), field(6), field(18), field(16)],
        compiler_params=pltpu.CompilerParams(vmem_limit_bytes=VMEM_LIMIT),
        name="operators",
    )(*arguments)


def final_kernel(
    table_ref, source_ref, own_ref, applied_ref, force_ref, image_ref, image2_ref, pimage_ref, pimage2_ref,
    temperature_ref, adjoint_ref, displacement_ref, displacement_adjoint_ref, thermal_ref, elastic_ref,
):
    table = table_ref[...].reshape(table_ref.shape[0], WIDTH)

    def column(k):
        return table[:, k : k + 1]

    def total(value):
        return jnp.sum(value, axis=0, keepdims=True)

    step0 = total(column(0)) / total(column(1))
    step1 = total(column(2)) / total(column(3))

    def solve(first):
        n_all, m_all = column(first), column(first + 1)
        n, m = total(n_all), total(m_all)
        theta = m / n
        local = jnp.where(n_all > 0.0, m_all / jnp.where(n_all > 0.0, n_all, 1.0), 0.0)
        gap = local - theta
        s = total(column(first + 2) + gap * gap * n_all)
        t = total(column(first + 3) + gap * column(first + 4) + gap * gap * m_all)
        alpha0 = n / m
        beta = s * alpha0 * alpha0 / n
        alpha1 = s / (t - s * s / m)
        return alpha0, beta, alpha1

    def outcome(coefficients, b, w, u):
        alpha0, beta, alpha1 = coefficients
        r = b - alpha0 * w
        x = alpha0 * b + alpha1 * (r + beta * b)
        r = r - alpha1 * ((w - alpha0 * u) + beta * w)
        return x, r

    forward, adjoint = solve(4), solve(9)
    for layer in range(source_ref.shape[0]):
        source = source_ref[layer]
        port = own_ref[source_ref.shape[0] + layer]
        temperature_ref[layer] = step0 * source
        adjoint_ref[layer] = step1 * port
        thermal_ref[0, layer] = source - step0 * applied_ref[0, layer]
        thermal_ref[1, layer] = port - step1 * applied_ref[1, layer]
        for k in range(3):
            x, r = outcome(forward, force_ref[k, layer], image_ref[k, layer], image2_ref[k, layer])
            displacement_ref[k, layer] = step0 * x
            elastic_ref[0, k, layer] = step0 * r
        x, r = outcome(adjoint, port, pimage_ref[layer], pimage2_ref[layer])
        for k in range(3):
            displacement_adjoint_ref[k, layer] = PORT_DIRECTION[k] * x
            elastic_ref[1, k, layer] = PORT_DIRECTION[k] * r


def final_stage(arguments, layers, height):
    own = (layers, height, WIDTH)
    shapes = [own, own, (3,) + own, (3,) + own, (2,) + own, (2, 3) + own]
    vmem = pl.BlockSpec(memory_space=pltpu.VMEM)
    return pl.pallas_call(
        final_kernel,
        out_shape=[jax.ShapeDtypeStruct(s, F32) for s in shapes],
        in_specs=[vmem] * len(arguments),
        out_specs=[vmem] * len(shapes),
        compiler_params=pltpu.CompilerParams(vmem_limit_bytes=VMEM_LIMIT),
        name="outputs",
    )(*arguments)


def per_device(density, anchor_mask, port_mask, heater_owner, heater_cell, heater_power):
    layers, height, _ = density.shape
    count = lax.axis_size("gx")
    devices = count * lax.axis_size("gz")
    heaters = tuple(a.reshape(1, -1) for a in (heater_owner, heater_cell, heater_power))
    heaters = tuple(pltpu.with_memory_space_constraint(a, pltpu.HBM) for a in (density, anchor_mask, port_mask) + heaters)
    first, second, far_one, far_two, own, entries = prepare(heaters, count)
    first = lax.ppermute(first, "gx", swap_pairs(count, 0, 1))
    second = lax.ppermute(second, "gx", swap_pairs(count, 1, 1))
    entries = lax.all_to_all(entries, "gx", 0, 0, tiled=True)
    far_one = lax.ppermute(far_one, "gx", swap_pairs(count, 0, 2))
    far_two = lax.ppermute(far_two, "gx", swap_pairs(count, 2, 2))
    far = jnp.concatenate([far_one, far_two])
    own_z = across_z(own)
    first_z = across_z(first)
    second_z = across_z(second)
    far_z = across_z(far)
    heat = scatter_heat(entries, layers, height)
    heat_z = across_z(heat)
    source, applied, force, image, image2, pimage, pimage2, sums = main_stage(
        (own, own_z, first, first_z, second, second_z, far, far_z, heat, heat_z),
        devices, layers, height,
    )
    table = lax.all_to_all(sums, ("gx", "gz"), 0, 0, tiled=True)
    return tuple(
        final_stage(
            (table, source, own, applied, force, image, image2, pimage, pimage2), layers, height
        )
    )


def solution(mesh):
    in_specs = (
        P("gx", None, "gz"),
        P("gx", None, "gz"),
        P("gx", None, "gz"),
        P("gx", "gz", None, None),
        P("gx", "gz", None),
        P("gx", "gz", None),
    )
    out_specs = (
        P("gx", None, "gz"),
        P("gx", None, "gz"),
        P(None, "gx", None, "gz"),
        P(None, "gx", None, "gz"),
        P(None, "gx", None, "gz"),
        P(None, None, "gx", None, "gz"),
    )
    return jax.shard_map(per_device, mesh=mesh, in_specs=in_specs, out_specs=out_specs, check_vma=False)
```

```python
import functools

import jax
import jax.numpy as jnp
from jax import lax
from jax.experimental import pallas as pl
from jax.experimental.pallas import tpu as pltpu
from jax.sharding import PartitionSpec as P


KAPPA_MIN = 0.05
MODULUS_MINIMUM = 0.02
CONVECTION = 0.2
PENALTY = 10.0
JOULE_GAIN = 1.0
SIGMA_MIN = 0.1
EXPANSION = 4.0
PORT_DIRECTION = (1.0, 0.5, -0.5)


HALO = 3
WIDTH = 128
EDGE = 8
VMEM_LIMIT = 16 << 20
F32 = jnp.float32


def swap_pairs(count, offset, distance):
    pairs = []
    for low in range(offset, count - distance):
        if ((low - offset) // distance) % 2 == 0:
            pairs += [(low, low + distance), (low + distance, low)]
    return pairs


def across_z(values):
    count = lax.axis_size("gz")
    if count == 2:
        return lax.ppermute(values, "gz", [(0, 1), (1, 0)])
    upper = lax.ppermute(values, "gz", [(i + 1, i) for i in range(count - 1)])
    lower = lax.ppermute(values, "gz", [(i, i + 1) for i in range(count - 1)])
    lanes = lax.broadcasted_iota(jnp.int32, values.shape, values.ndim - 1)
    return jnp.where(lanes < WIDTH // 2, upper, lower)


def prepare_kernel(
    density_hbm, anchor_hbm, port_hbm, owner_hbm, cell_hbm, power_hbm,
    first_ref, second_ref, far_one_ref, far_two_ref, own_ref, entries_ref,
    density_ref, anchor_ref, port_ref, owner_ref, cell_ref, power_ref, arrived,
):
    layers = density_ref.shape[0]
    sources = (owner_hbm, cell_hbm, power_hbm, density_hbm, port_hbm, anchor_hbm)
    targets = (owner_ref, cell_ref, power_ref, density_ref, port_ref, anchor_ref)
    copies = [
        pltpu.make_async_copy(source, target, arrived.at[k])
        for k, (source, target) in enumerate(zip(sources, targets))
    ]
    for copy in copies:
        copy.start()
    gx = lax.axis_index("gx")
    even = gx % 2 == 0
    low_pair = gx % 4 < 2
    for copy in copies[:3]:
        copy.wait()
    owner = owner_ref[...].astype(F32)
    cell = cell_ref[...].astype(F32)
    power = power_ref[...]
    for k in range(entries_ref.shape[0]):
        entries_ref[k, 0:1] = owner
        entries_ref[k, 1:2] = cell
        entries_ref[k, 2:3] = power
    copies[3].wait()
    for layer in range(layers):
        density = density_ref[layer]
        for ref in (first_ref, second_ref, own_ref):
            ref[layer] = density
    below, above = density_ref[0], density_ref[layers - 1]
    far_one_ref[0] = jnp.where(low_pair, above, below)
    far_two_ref[0] = jnp.where(low_pair, below, above)
    copies[4].wait()
    for layer in range(layers):
        port = port_ref[layer].astype(F32)
        for ref in (first_ref, second_ref, own_ref):
            ref[layers + layer] = port
    copies[5].wait()
    for layer in range(layers):
        own_ref[2 * layers + layer] = anchor_ref[layer].astype(F32)
    below, above = anchor_ref[0].astype(F32), anchor_ref[layers - 1].astype(F32)
    first_ref[2 * layers] = jnp.where(even, above, below)
    second_ref[2 * layers] = jnp.where(even, below, above)


def prepare(arguments, sources):
    layers, height, _ = arguments[0].shape
    plane = (height, WIDTH)
    shapes = [
        (2 * layers + 1,) + plane, (2 * layers + 1,) + plane, (1,) + plane, (1,) + plane,
        (3 * layers,) + plane, (sources, 3, arguments[-1].shape[1]),
    ]
    return pl.pallas_call(
        prepare_kernel,
        out_shape=[jax.ShapeDtypeStruct(s, F32) for s in shapes],
        in_specs=[pl.BlockSpec(memory_space=pltpu.HBM)] * len(arguments),
        out_specs=[pl.BlockSpec(memory_space=pltpu.VMEM)] * len(shapes),
        scratch_shapes=[pltpu.VMEM(a.shape, a.dtype) for a in arguments]
        + [pltpu.SemaphoreType.DMA((len(arguments),))],
        compiler_params=pltpu.CompilerParams(vmem_limit_bytes=VMEM_LIMIT),
        name="prepare",
    )(*arguments)


def heater_kernel(entries_ref, heat_ref, far_ref, rows_ref, lanes_ref, total_ref, *, layers, height, block):
    sources = entries_ref.shape[0]
    entries = entries_ref.shape[2]
    slabs = layers + 2 * HALO
    base = lax.axis_index("gx") * layers - HALO
    row_ids = lax.broadcasted_iota(jnp.int32, (slabs * height, entries), 0)
    lane_ids = lax.broadcasted_iota(jnp.int32, (WIDTH, entries), 0)
    plane = height * WIDTH

    def one_block(start):
        for k in range(block):
            table = entries_ref[start + k]
            owner = table[0:1].astype(jnp.int32)
            cell = table[1:2].astype(jnp.int32)
            power = table[2:3]
            rest = cell % plane
            row = (owner * layers + cell // plane - base) * height + rest // WIDTH
            lane = rest % WIDTH
            high = power.astype(jnp.bfloat16).astype(F32)
            low = power - high
            here = slice(k * entries, (k + 1) * entries)
            rows_ref[:, here] = jnp.where(row_ids == row, 1.0, 0.0).astype(jnp.bfloat16)
            match = lane_ids == lane
            lanes_ref[0:WIDTH, here] = jnp.where(match, high, 0.0).astype(jnp.bfloat16)
            lanes_ref[WIDTH:, here] = jnp.where(match, low, 0.0).astype(jnp.bfloat16)
        return lax.dot_general(
            rows_ref[...], lanes_ref[...], (((1,), (1,)), ((), ())), preferred_element_type=F32
        )

    total = one_block(0)
    if sources > block:
        total_ref[...] = total

        @pl.loop(1, sources // block)
        def _(step):
            total_ref[...] += one_block(step * block)

        total = total_ref[...]
    heat = total[:, :WIDTH] + total[:, WIDTH:]
    heat = heat.reshape(slabs, height, WIDTH)
    heat_ref[...] = heat[1 : slabs - 1]
    far_ref[0] = heat[0]
    far_ref[1] = heat[slabs - 1]


def scatter_heat(entries, layers, height):
    sources, _, count = entries.shape
    block = min(sources, 16)
    slabs = layers + 2 * HALO
    return pl.pallas_call(
        functools.partial(heater_kernel, layers=layers, height=height, block=block),
        out_shape=[jax.ShapeDtypeStruct((k, height, WIDTH), F32) for k in (slabs - 2, 2)],
        in_specs=[pl.BlockSpec(memory_space=pltpu.VMEM)],
        out_specs=[pl.BlockSpec(memory_space=pltpu.VMEM)] * 2,
        scratch_shapes=[
            pltpu.VMEM((slabs * height, block * count), jnp.bfloat16),
            pltpu.VMEM((2 * WIDTH, block * count), jnp.bfloat16),
            pltpu.VMEM((slabs * height, 2 * WIDTH), F32),
        ],
        compiler_params=pltpu.CompilerParams(vmem_limit_bytes=VMEM_LIMIT),
        name="heater_scatter",
    )(entries)


def main_kernel(
    own_ref, own_z_ref, first_ref, first_z_ref, second_ref, second_z_ref,
    far_one_ref, far_two_ref, heat_ref, heat_z_ref, heat_far_ref,
    source_ref, applied_ref, force_ref, image_ref, image2_ref, pimage_ref, pimage2_ref, sums_ref,
    cub, stress, src, prt, force, image,
):
    height = own_ref.shape[1]
    gx = lax.axis_index("gx")
    gz = lax.axis_index("gz")
    last_x = lax.axis_size("gx") - 1
    last_z = lax.axis_size("gz") - 1
    even = gx % 2 == 0
    low_pair = gx % 4 < 2

    def flag(condition):
        return jnp.where(condition, 1.0, 0.0).astype(F32)

    tile = (height, WIDTH)
    lanes = lax.broadcasted_iota(jnp.int32, tile, 1)
    is_last = lanes == WIDTH - 1
    is_first = lanes == 0
    z_valid = jnp.where(lanes < WIDTH // 2, flag(gz < last_z), flag(gz > 0))
    x_valid = [
        flag(gx >= 2), flag(gx >= 1), flag(gx >= 1), None, None,
        flag(gx < last_x), flag(gx < last_x), flag(gx < last_x - 1),
    ]
    symmetry = flag(gx > 0)

    def masked(side, layer, value):
        if side:
            value = value * z_valid
        if x_valid[layer] is not None:
            value = value * x_valid[layer]
        return value

    def load(ref, side, layer, shift=0):
        return ref[side, layer, EDGE + shift : EDGE + shift + height, :]

    def store(ref, side, layer, value):
        ref[side, layer, EDGE : EDGE + height, :] = value

    def z_up(pair):
        a, b = (pltpu.roll(v, WIDTH - 1, 1) for v in pair)
        return jnp.where(is_last, b, a), jnp.where(is_last, a, b)

    def z_down(pair):
        a, b = (pltpu.roll(v, 1, 1) for v in pair)
        return jnp.where(is_first, b, a), jnp.where(is_first, a, b)

    edge_rows = jnp.zeros((EDGE, WIDTH), F32)
    for ref in (cub, stress, src, prt, force, image):
        for side in range(2):
            for layer in range(ref.shape[1]):
                ref[side, layer, 0:EDGE, :] = edge_rows
                ref[side, layer, EDGE + height :, :] = edge_rows

    def lower(side, k):
        a, b = (first_z_ref, second_z_ref) if side else (first_ref, second_ref)
        return jnp.where(even, b[k], a[k])

    def upper(side, k):
        a, b = (first_z_ref, second_z_ref) if side else (first_ref, second_ref)
        return jnp.where(even, a[k], b[k])

    def far(low):
        one, two = far_one_ref[0], far_two_ref[0]
        return jnp.where(low_pair, two, one) if low else jnp.where(low_pair, one, two)

    def density_of(side, layer):
        if layer == 0:
            return far(True)
        if layer == 7:
            return far(False)
        if layer in (1, 2):
            return lower(side, layer - 1)
        if layer in (5, 6):
            return upper(side, layer - 5)
        return (own_z_ref if side else own_ref)[layer - 3]

    def port_of(side, layer):
        if layer in (1, 2):
            return lower(side, layer + 1)
        if layer in (5, 6):
            return upper(side, layer - 3)
        return (own_z_ref if side else own_ref)[layer - 1]

    def anchor_of(side, layer):
        if layer == 2:
            return lower(side, 4)
        if layer == 5:
            return upper(side, 4)
        return (own_z_ref if side else own_ref)[layer + 1]

    for layer in range(8):
        outermost = layer in (0, 7)
        for side in range(1 if outermost else 2):
            d = masked(side, layer, density_of(side, layer))
            c = d * d * d
            heat = heat_far_ref[layer // 7] if outermost else (heat_z_ref if side else heat_ref)[layer - 1]
            s = masked(side, layer, JOULE_GAIN * (SIGMA_MIN + c) + heat)
            store(cub, side, layer, c)
            store(stress, side, layer, (MODULUS_MINIMUM + c) * s)
            if 2 <= layer <= 5:
                store(src, side, layer - 2, s)
            if side == 0 and layer in (3, 4):
                source_ref[layer - 3] = s
            if 1 <= layer <= 6:
                store(prt, side, layer - 1, masked(side, layer, port_of(side, layer)))
    store(stress, 1, 0, jnp.zeros(tile, F32))
    store(stress, 1, 7, jnp.zeros(tile, F32))
    for side in range(2):
        for layer, block in ((0, 1), (2, 0)):
            mirrored = jnp.where(gx == block, load(stress, side, layer + 1), load(stress, side, layer))
            store(stress, side, layer, mirrored)

    half = EXPANSION * 0.5
    for layer in range(1, 7):
        pair = [load(stress, side, layer) for side in range(2)]
        up, down = z_up(pair), z_down(pair)
        for side in range(2):
            parts = (
                load(stress, side, layer + 1) - load(stress, side, layer - 1),
                load(stress, side, layer, 1) - load(stress, side, layer, -1),
                up[side] - down[side],
            )
            for k in range(3):
                value = masked(side, layer, half * parts[k])
                store(force, side, k * 6 + layer - 1, value)
                if side == 0 and layer in (3, 4):
                    force_ref[k, layer - 3] = value

    def face(a, b):
        return MODULUS_MINIMUM + 0.5 * (a + b)

    sums = {}

    def accumulate(name, value):
        value = jnp.sum(value.reshape(height // 8, 8, WIDTH), axis=0)
        sums[name] = value if name not in sums else sums[name] + value

    def weights_of(layer):
        pair = [load(cub, side, layer) for side in range(2)]
        up, down = z_up(pair), z_down(pair)
        result = []
        for side in range(2):
            c = pair[side]
            x_low = face(load(cub, side, layer - 1), c)
            if layer == 3:
                x_low = x_low * symmetry
            result.append(
                (
                    x_low,
                    face(load(cub, side, layer + 1), c),
                    face(load(cub, side, layer, -1), c),
                    face(load(cub, side, layer, 1), c),
                    face(down[side], c),
                    face(up[side], c),
                )
            )
        return result

    def differences(ref, index, sides):
        pair = [load(ref, side, index) for side in range(2)]
        up, down = z_up(pair), z_down(pair)
        result = []
        for side in sides:
            v = pair[side]
            result.append(
                (
                    v,
                    (
                        v - load(ref, side, index - 1),
                        v - load(ref, side, index + 1),
                        v - load(ref, side, index, -1),
                        v - load(ref, side, index, 1),
                        v - down[side],
                        v - up[side],
                    ),
                )
            )
        return result

    def weighted(weights, parts):
        total = weights[0] * parts[0]
        for w, p in zip(weights[1:], parts[1:]):
            total = total + w * p
        return total

    own_weights, own_anchor = {}, {}
    spread = KAPPA_MIN - MODULUS_MINIMUM
    for layer in range(2, 6):
        weights = weights_of(layer)
        anchors = [PENALTY * anchor_of(side, layer) for side in range(2)]
        own = layer in (3, 4)
        if own:
            own_weights[layer], own_anchor[layer] = weights[0], anchors[0]
        for k in range(4):
            ref, index = (force, k * 6 + layer - 1) if k < 3 else (prt, layer - 1)
            for side, (v, parts) in enumerate(differences(ref, index, range(2))):
                flux = weighted(weights[side], parts)
                value = masked(side, layer, flux + anchors[side] * v)
                store(image, side, k * 4 + layer - 2, value)
                if own and side == 0:
                    if k < 3:
                        image_ref[k, layer - 3] = value
                        accumulate("n0", v * v)
                        accumulate("m0", v * value)
                    else:
                        pimage_ref[layer - 3] = value
                        accumulate("n1", v * v)
                        accumulate("m1", v * value)
                        first = parts[0] * symmetry if layer == 3 else parts[0]
                        plain = first + parts[1] + parts[2] + parts[3] + parts[4] + parts[5]
                        heat_image = flux + spread * plain + CONVECTION * v
                        applied_ref[1, layer - 3] = heat_image
                        accumulate("k1", v * heat_image)
        if own:
            v, parts = differences(src, layer - 2, (0,))[0]
            heat_weights = [w + spread for w in weights[0]]
            if layer == 3:
                heat_weights[0] = weights[0][0] + spread * symmetry
            heat_image = weighted(heat_weights, parts) + CONVECTION * v
            applied_ref[0, layer - 3] = heat_image
            accumulate("k", v * heat_image)
            accumulate("q", v * v)

    def total(value):
        return jnp.sum(jnp.sum(value, axis=0, keepdims=True), axis=1, keepdims=True)

    final = {name: total(sums[name]) for name in ("n0", "m0", "n1", "m1", "k", "q", "k1")}
    shift = []
    for member in range(2):
        n, m = final["n%d" % member], final["m%d" % member]
        shift.append(jnp.where(n > 0.0, m / jnp.where(n > 0.0, n, 1.0), 0.0))
    for layer in (3, 4):
        for k in range(4):
            v, parts = differences(image, k * 4 + layer - 2, (0,))[0]
            value = weighted(own_weights[layer], parts) + own_anchor[layer] * v
            if k < 3:
                image2_ref[k, layer - 3] = value
                start = load(force, 0, k * 6 + layer - 1)
            else:
                pimage2_ref[layer - 3] = value
                start = load(prt, 0, layer - 1)
            theta = shift[k // 3]
            r = v - theta * start
            y = value - theta * v
            accumulate("s%d" % (k // 3), r * r)
            accumulate("t%d" % (k // 3), r * y)
            accumulate("c%d" % (k // 3), start * y)
    for member in range(2):
        for name in "stc":
            final[name + str(member)] = total(sums[name + str(member)])
    columns = (
        final["q"], final["k"], final["n1"], final["k1"],
        final["n0"], final["m0"], final["s0"], final["t0"], final["c0"] + final["s0"],
        final["n1"], final["m1"], final["s1"], final["t1"], final["c1"] + final["s1"],
    )
    lane = lax.broadcasted_iota(jnp.int32, (1, WIDTH), 1)
    row = jnp.zeros((1, WIDTH), F32)
    for k, column in enumerate(columns):
        row = jnp.where(lane == k, column, row)
    sums_ref[...] = jnp.broadcast_to(row[None], sums_ref.shape)


def main_stage(arguments, devices, layers, height):
    own = (layers, height, WIDTH)
    vectors = (3,) + own
    shapes = [own, (2,) + own, vectors, vectors, vectors, own, own, (devices, 1, WIDTH)]

    def field(count):
        return pltpu.VMEM((2, count, height + 2 * EDGE, WIDTH), F32)

    vmem = pl.BlockSpec(memory_space=pltpu.VMEM)
    return pl.pallas_call(
        main_kernel,
        out_shape=[jax.ShapeDtypeStruct(s, F32) for s in shapes],
        in_specs=[vmem] * len(arguments),
        out_specs=[vmem] * len(shapes),
        scratch_shapes=[field(8), field(8), field(4), field(6), field(18), field(16)],
        compiler_params=pltpu.CompilerParams(vmem_limit_bytes=VMEM_LIMIT),
        name="operators",
    )(*arguments)


def final_kernel(
    table_ref, source_ref, own_ref, applied_ref, force_ref, image_ref, image2_ref, pimage_ref, pimage2_ref,
    temperature_ref, adjoint_ref, displacement_ref, displacement_adjoint_ref, thermal_ref, elastic_ref,
):
    table = table_ref[...].reshape(table_ref.shape[0], WIDTH)

    def column(k):
        return table[:, k : k + 1]

    def total(value):
        return jnp.sum(value, axis=0, keepdims=True)

    step0 = total(column(0)) / total(column(1))
    step1 = total(column(2)) / total(column(3))

    def solve(first):
        n_all, m_all = column(first), column(first + 1)
        n, m = total(n_all), total(m_all)
        theta = m / n
        local = jnp.where(n_all > 0.0, m_all / jnp.where(n_all > 0.0, n_all, 1.0), 0.0)
        gap = local - theta
        s = total(column(first + 2) + gap * gap * n_all)
        t = total(column(first + 3) + gap * column(first + 4) + gap * gap * m_all)
        alpha0 = n / m
        beta = s * alpha0 * alpha0 / n
        alpha1 = s / (t - s * s / m)
        return alpha0, beta, alpha1

    def outcome(coefficients, b, w, u):
        alpha0, beta, alpha1 = coefficients
        r = b - alpha0 * w
        x = alpha0 * b + alpha1 * (r + beta * b)
        r = r - alpha1 * ((w - alpha0 * u) + beta * w)
        return x, r

    forward, adjoint = solve(4), solve(9)
    for layer in range(source_ref.shape[0]):
        source = source_ref[layer]
        port = own_ref[source_ref.shape[0] + layer]
        temperature_ref[layer] = step0 * source
        adjoint_ref[layer] = step1 * port
        thermal_ref[0, layer] = source - step0 * applied_ref[0, layer]
        thermal_ref[1, layer] = port - step1 * applied_ref[1, layer]
        for k in range(3):
            x, r = outcome(forward, force_ref[k, layer], image_ref[k, layer], image2_ref[k, layer])
            displacement_ref[k, layer] = step0 * x
            elastic_ref[0, k, layer] = step0 * r
        x, r = outcome(adjoint, port, pimage_ref[layer], pimage2_ref[layer])
        for k in range(3):
            displacement_adjoint_ref[k, layer] = PORT_DIRECTION[k] * x
            elastic_ref[1, k, layer] = PORT_DIRECTION[k] * r


def final_stage(arguments, layers, height):
    own = (layers, height, WIDTH)
    shapes = [own, own, (3,) + own, (3,) + own, (2,) + own, (2, 3) + own]
    vmem = pl.BlockSpec(memory_space=pltpu.VMEM)
    return pl.pallas_call(
        final_kernel,
        out_shape=[jax.ShapeDtypeStruct(s, F32) for s in shapes],
        in_specs=[vmem] * len(arguments),
        out_specs=[vmem] * len(shapes),
        compiler_params=pltpu.CompilerParams(vmem_limit_bytes=VMEM_LIMIT),
        name="outputs",
    )(*arguments)


def per_device(density, anchor_mask, port_mask, heater_owner, heater_cell, heater_power):
    layers, height, _ = density.shape
    count = lax.axis_size("gx")
    devices = count * lax.axis_size("gz")
    heaters = tuple(a.reshape(1, -1) for a in (heater_owner, heater_cell, heater_power))
    heaters = tuple(pltpu.with_memory_space_constraint(a, pltpu.HBM) for a in (density, anchor_mask, port_mask) + heaters)
    first, second, far_one, far_two, own, entries = prepare(heaters, count)
    first = lax.ppermute(first, "gx", swap_pairs(count, 0, 1))
    second = lax.ppermute(second, "gx", swap_pairs(count, 1, 1))
    entries = lax.all_to_all(entries, "gx", 0, 0, tiled=True)
    far_one = lax.ppermute(far_one, "gx", swap_pairs(count, 0, 2))
    far_two = lax.ppermute(far_two, "gx", swap_pairs(count, 2, 2))
    own_z = across_z(own)
    first_z = across_z(first)
    second_z = across_z(second)
    heat, heat_far = scatter_heat(entries, layers, height)
    heat_z = across_z(heat)
    source, applied, force, image, image2, pimage, pimage2, sums = main_stage(
        (own, own_z, first, first_z, second, second_z, far_one, far_two, heat, heat_z, heat_far),
        devices, layers, height,
    )
    table = lax.all_to_all(sums, ("gx", "gz"), 0, 0, tiled=True)
    return tuple(
        final_stage(
            (table, source, own, applied, force, image, image2, pimage, pimage2), layers, height
        )
    )


def solution(mesh):
    in_specs = (
        P("gx", None, "gz"),
        P("gx", None, "gz"),
        P("gx", None, "gz"),
        P("gx", "gz", None, None),
        P("gx", "gz", None),
        P("gx", "gz", None),
    )
    out_specs = (
        P("gx", None, "gz"),
        P("gx", None, "gz"),
        P(None, "gx", None, "gz"),
        P(None, "gx", None, "gz"),
        P(None, "gx", None, "gz"),
        P(None, None, "gx", None, "gz"),
    )
    return jax.shard_map(per_device, mesh=mesh, in_specs=in_specs, out_specs=out_specs, check_vma=False)
```

```python
import functools

import jax
import jax.numpy as jnp
from jax import lax
from jax.experimental import pallas as pl
from jax.experimental.pallas import tpu as pltpu
from jax.sharding import PartitionSpec as P


KAPPA_MIN = 0.05
MODULUS_MINIMUM = 0.02
CONVECTION = 0.2
PENALTY = 10.0
JOULE_GAIN = 1.0
SIGMA_MIN = 0.1
EXPANSION = 4.0
PORT_DIRECTION = (1.0, 0.5, -0.5)


HALO = 3
WIDTH = 128
EDGE = 8
STRIP = 8
VMEM_LIMIT = 16 << 20
F32 = jnp.float32


def swap_pairs(count, offset, distance):
    pairs = []
    for low in range(offset, count - distance):
        if ((low - offset) // distance) % 2 == 0:
            pairs += [(low, low + distance), (low + distance, low)]
    return pairs


def across_z(values):
    count = lax.axis_size("gz")
    if count == 2:
        return lax.ppermute(values, "gz", [(0, 1), (1, 0)])
    upper = lax.ppermute(values, "gz", [(i + 1, i) for i in range(count - 1)])
    lower = lax.ppermute(values, "gz", [(i, i + 1) for i in range(count - 1)])
    lanes = lax.broadcasted_iota(jnp.int32, values.shape, values.ndim - 1)
    return jnp.where(lanes < WIDTH // 2, upper, lower)


def prepare_kernel(
    density_hbm, anchor_hbm, port_hbm, owner_hbm, cell_hbm, power_hbm,
    first_ref, second_ref, far_one_ref, far_two_ref, own_ref, entries_hbm,
    density_ref, anchor_ref, port_ref, owner_ref, cell_ref, power_ref, entries_ref, arrived,
):
    layers = density_ref.shape[0]
    sources = (owner_hbm, cell_hbm, power_hbm, density_hbm, port_hbm, anchor_hbm)
    targets = (owner_ref, cell_ref, power_ref, density_ref, port_ref, anchor_ref)
    copies = [
        pltpu.make_async_copy(source, target, arrived.at[k])
        for k, (source, target) in enumerate(zip(sources, targets))
    ]
    for copy in copies:
        copy.start()
    gx = lax.axis_index("gx")
    even = gx % 2 == 0
    low_pair = gx % 4 < 2
    for copy in copies[:3]:
        copy.wait()
    owner = owner_ref[...].astype(F32)
    cell = cell_ref[...].astype(F32)
    power = power_ref[...]
    for k in range(entries_ref.shape[0]):
        entries_ref[k, 0:1] = owner
        entries_ref[k, 1:2] = cell
        entries_ref[k, 2:3] = power
    leaving = pltpu.make_async_copy(entries_ref, entries_hbm, arrived.at[len(copies)])
    leaving.start()
    copies[3].wait()
    for layer in range(layers):
        density = density_ref[layer]
        for ref in (first_ref, second_ref, own_ref):
            ref[layer] = density
    below, above = density_ref[0], density_ref[layers - 1]
    far_one_ref[0] = jnp.where(low_pair, above, below)
    far_two_ref[0] = jnp.where(low_pair, below, above)
    copies[4].wait()
    for layer in range(layers):
        port = port_ref[layer].astype(F32)
        for ref in (first_ref, second_ref, own_ref):
            ref[layers + layer] = port
    copies[5].wait()
    for layer in range(layers):
        own_ref[2 * layers + layer] = anchor_ref[layer].astype(F32)
    below, above = anchor_ref[0].astype(F32), anchor_ref[layers - 1].astype(F32)
    first_ref[2 * layers] = jnp.where(even, above, below)
    second_ref[2 * layers] = jnp.where(even, below, above)
    leaving.wait()


def prepare(arguments, sources):
    layers, height, _ = arguments[0].shape
    plane = (height, WIDTH)
    shapes = [
        (2 * layers + 1,) + plane, (2 * layers + 1,) + plane, (1,) + plane, (1,) + plane,
        (3 * layers,) + plane, (sources, 3, arguments[-1].shape[1]),
    ]
    return pl.pallas_call(
        prepare_kernel,
        out_shape=[jax.ShapeDtypeStruct(s, F32) for s in shapes],
        in_specs=[pl.BlockSpec(memory_space=pltpu.HBM)] * len(arguments),
        out_specs=[pl.BlockSpec(memory_space=pltpu.VMEM)] * (len(shapes) - 1)
        + [pl.BlockSpec(memory_space=pltpu.HBM)],
        scratch_shapes=[pltpu.VMEM(a.shape, a.dtype) for a in arguments]
        + [pltpu.VMEM(shapes[-1], F32), pltpu.SemaphoreType.DMA((len(arguments) + 1,))],
        compiler_params=pltpu.CompilerParams(vmem_limit_bytes=VMEM_LIMIT),
        name="prepare",
    )(*arguments)


def heater_kernel(entries_ref, heat_ref, far_ref, rows_ref, lanes_ref, *total_refs, layers, height, block):
    sources = entries_ref.shape[0]
    entries = entries_ref.shape[2]
    slabs = layers + 2 * HALO
    base = lax.axis_index("gx") * layers - HALO
    plane_bits = (height * WIDTH).bit_length() - 1
    lane_bits = WIDTH.bit_length() - 1
    height_bits = height.bit_length() - 1
    group = slabs * height
    row_ids = lax.broadcasted_iota(jnp.int32, (group, entries), 0)
    lane_ids = lax.broadcasted_iota(jnp.int32, (WIDTH, entries), 0)

    def one_block(start, keep):
        rows = []
        for k in range(block):
            table = entries_ref[start + k]
            owner = table[0:1].astype(jnp.int32)
            cell = table[1:2].astype(jnp.int32)
            power = table[2:3]
            slab = owner * layers + (cell >> plane_bits) - base
            rows.append((slab << height_bits) + ((cell >> lane_bits) & (height - 1)))
            high = power.astype(jnp.bfloat16).astype(F32)
            low = power - high
            here = slice(k * entries, (k + 1) * entries)
            match = lane_ids == (cell & (WIDTH - 1))
            lanes_ref[0:WIDTH, here] = jnp.where(match, high, 0.0).astype(jnp.bfloat16)
            lanes_ref[WIDTH:, here] = jnp.where(match, low, 0.0).astype(jnp.bfloat16)
            rows_ref[:, here] = jnp.where(row_ids == rows[k], 1.0, 0.0).astype(jnp.bfloat16)
        both = None
        width = block * entries // 1
        for k in range(1):
            here = slice(k * width, (k + 1) * width)
            part = lax.dot_general(
                rows_ref[:, here], lanes_ref[:, here], (((1,), (1,)), ((), ())), preferred_element_type=F32
            )
            both = part if both is None else both + part
        keep(0, both[:, :WIDTH] + both[:, WIDTH:])

    def write(first, part):
        for k in range(group // height):
            slab = first // height + k
            value = part[k * height : (k + 1) * height]
            if slab in (0, slabs - 1):
                far_ref[slab // (slabs - 1)] = value
            else:
                heat_ref[slab - 1] = value

    if sources == block:
        one_block(0, write)
        return
    total_ref = total_refs[0]
    total_ref[...] = jnp.zeros_like(total_ref)

    def add(first, part):
        total_ref[first : first + group, :] += part

    @pl.loop(0, sources // block)
    def _(step):
        one_block(step * block, add)

    for first in range(0, slabs * height, group):
        write(first, total_ref[first : first + group, :])


def scatter_heat(entries, layers, height):
    sources, _, count = entries.shape
    block = min(sources, 16)
    slabs = layers + 2 * HALO
    if height & (height - 1) or sources % block:
        raise ValueError("unsupported sizes")
    scratch = [
        pltpu.VMEM((slabs * height, block * count), jnp.bfloat16),
        pltpu.VMEM((2 * WIDTH, block * count), jnp.bfloat16),
    ]
    if sources > block:
        scratch.append(pltpu.VMEM((slabs * height, WIDTH), F32))
    return pl.pallas_call(
        functools.partial(heater_kernel, layers=layers, height=height, block=block),
        out_shape=[jax.ShapeDtypeStruct((k, height, WIDTH), F32) for k in (slabs - 2, 2)],
        in_specs=[pl.BlockSpec(memory_space=pltpu.VMEM)],
        out_specs=[pl.BlockSpec(memory_space=pltpu.VMEM)] * 2,
        scratch_shapes=scratch,
        compiler_params=pltpu.CompilerParams(vmem_limit_bytes=VMEM_LIMIT),
        name="heater_scatter",
    )(entries)


class Block:
    def __init__(self, height):
        gx, gz = lax.axis_index("gx"), lax.axis_index("gz")
        last_x, last_z = lax.axis_size("gx") - 1, lax.axis_size("gz") - 1

        def flag(condition):
            return jnp.where(condition, 1.0, 0.0).astype(F32)

        self.gx = gx
        self.height = height
        self.start = 0
        self.even = gx % 2 == 0
        self.low_pair = gx % 4 < 2
        lanes = lax.broadcasted_iota(jnp.int32, (STRIP, WIDTH), 1)
        self.is_last = lanes == WIDTH - 1
        self.is_first = lanes == 0
        self.z_valid = jnp.where(lanes < WIDTH // 2, flag(gz < last_z), flag(gz > 0))
        self.x_valid = [
            flag(gx >= 2), flag(gx >= 1), flag(gx >= 1), None, None,
            flag(gx < last_x), flag(gx < last_x), flag(gx < last_x - 1),
        ]
        self.symmetry = flag(gx > 0)
        self.sums = {}

    def strips(self):
        for start in range(0, self.height, STRIP):
            self.start = start
            yield start

    def masked(self, side, layer, value):
        if side:
            value = value * self.z_valid
        if self.x_valid[layer] is not None:
            value = value * self.x_valid[layer]
        return value

    def load(self, ref, side, layer, shift=0):
        first = EDGE + self.start + shift
        return ref[side, layer, first : first + STRIP, :]

    def store(self, ref, side, layer, value):
        first = EDGE + self.start
        ref[side, layer, first : first + STRIP, :] = value

    def read(self, ref, *index):
        return ref[index + (slice(self.start, self.start + STRIP), slice(None))]

    def write(self, ref, value, *index):
        ref[index + (slice(self.start, self.start + STRIP), slice(None))] = value

    def clear_edges(self, *refs):
        edge_rows = jnp.zeros((EDGE, WIDTH), F32)
        for ref in refs:
            for side in range(2):
                for layer in range(ref.shape[1]):
                    ref[side, layer, 0:EDGE, :] = edge_rows
                    ref[side, layer, EDGE + self.height :, :] = edge_rows

    def z_pair(self, ref, layer, side):
        value, other = self.load(ref, side, layer), self.load(ref, 1 - side, layer)
        down = pltpu.roll(jnp.where(self.is_last, other, value), 1, 1)
        up = pltpu.roll(jnp.where(self.is_first, other, value), WIDTH - 1, 1)
        return value, down, up

    def pick(self, own, first, second, layer, own_tile, near_tile):
        if layer in (3, 4):
            return self.read(own, own_tile + layer - 3)
        one, two = (second, first) if layer < 3 else (first, second)
        return jnp.where(self.even, self.read(one, near_tile), self.read(two, near_tile))

    def weights_of(self, cub, layer, side):
        def face(a, b):
            return MODULUS_MINIMUM + 0.5 * (a + b)

        index = layer - 1
        c, down, up = self.z_pair(cub, index, side)
        x_low = face(self.load(cub, side, index - 1), c)
        if layer == 3:
            x_low = x_low * self.symmetry
        return (
            x_low,
            face(self.load(cub, side, index + 1), c),
            face(self.load(cub, side, index, -1), c),
            face(self.load(cub, side, index, 1), c),
            face(down, c),
            face(up, c),
        )

    def differences(self, ref, index, side):
        v, down, up = self.z_pair(ref, index, side)
        parts = (
            v - self.load(ref, side, index - 1),
            v - self.load(ref, side, index + 1),
            v - self.load(ref, side, index, -1),
            v - self.load(ref, side, index, 1),
            v - down,
            v - up,
        )
        return v, parts

    def weighted(self, weights, parts):
        total = weights[0] * parts[0]
        for w, p in zip(weights[1:], parts[1:]):
            total = total + w * p
        return total

    def accumulate(self, name, value):
        value = jnp.sum(value.reshape(STRIP // 8, 8, WIDTH), axis=0)
        self.sums[name] = self.sums[name] + value if name in self.sums else value

    def total(self, name):
        return jnp.sum(jnp.sum(self.sums[name], axis=0, keepdims=True), axis=1, keepdims=True)

    def row(self, columns):
        lane = lax.broadcasted_iota(jnp.int32, (1, WIDTH), 1)
        row = jnp.zeros((1, WIDTH), F32)
        for k, column in columns.items():
            row = jnp.where(lane == k, column, row)
        return row


def ratio(m, n):
    return jnp.where(n > 0.0, m / jnp.where(n > 0.0, n, 1.0), 0.0)


SPREAD = KAPPA_MIN - MODULUS_MINIMUM


def port_kernel(
    own_ref, own_z_ref, first_ref, first_z_ref, second_ref, second_z_ref,
    cub, applied_ref, image_ref, image2_ref, row_ref,
    prt, image, kept,
):
    block = Block(own_ref.shape[1])
    block.clear_edges(cub, prt, image)
    near = ((own_ref, first_ref, second_ref), (own_z_ref, first_z_ref, second_z_ref))
    for layer in range(1, 7):
        tile = (layer - 1) % 4
        for side in range(2):
            for _ in block.strips():
                d = block.masked(side, layer, block.pick(*near[side], layer, 0, tile))
                block.store(cub, side, layer - 1, d * d * d)
                if 2 <= layer <= 5 or side == 0:
                    port = block.masked(side, layer, block.pick(*near[side], layer, 2, 2 + tile))
                    block.store(prt, side, layer - 1, port)
    for layer in range(2, 6):
        own = layer in (3, 4)
        for side in range(2 if own else 1):
            for _ in block.strips():
                weights = block.weights_of(cub, layer, side)
                v, parts = block.differences(prt, layer - 1, side)
                flux = block.weighted(weights, parts)
                anchor = PENALTY * block.pick(*near[side], layer, 4, 4)
                value = block.masked(side, layer, flux + anchor * v)
                block.store(image, side, layer - 2, value)
                if own and side == 0:
                    for k, weight in enumerate(weights):
                        block.write(kept, weight, layer - 3, k)
                    block.write(image_ref, value, layer - 3)
                    block.accumulate("n", v * v)
                    block.accumulate("m", v * value)
                    low = parts[0] * block.symmetry if layer == 3 else parts[0]
                    plain = low + parts[1] + parts[2] + parts[3] + parts[4] + parts[5]
                    heat_image = flux + SPREAD * plain + CONVECTION * v
                    block.write(applied_ref, heat_image, layer - 3)
                    block.accumulate("k", v * heat_image)
    n, m, k = (block.total(name) for name in "nmk")
    theta = ratio(m, n)
    for layer in (3, 4):
        for _ in block.strips():
            v, parts = block.differences(image, layer - 2, 0)
            weights = [block.read(kept, layer - 3, k6) for k6 in range(6)]
            anchor = PENALTY * block.read(own_ref, layer + 1)
            value = block.weighted(weights, parts) + anchor * v
            block.write(image2_ref, value, layer - 3)
            start = block.load(prt, 0, layer - 1)
            r = v - theta * start
            y = value - theta * v
            block.accumulate("s", r * r)
            block.accumulate("t", r * y)
            block.accumulate("c", start * y)
    s, t, c = (block.total(name) for name in "stc")
    row_ref[...] = block.row({2: n, 3: k, 9: n, 10: m, 11: s, 12: t, 13: c + s})


def force_kernel(
    own_ref, own_z_ref, first_ref, second_ref, far_one_ref, far_two_ref, heat_ref, heat_z_ref, heat_far_ref,
    cub, row_ref,
    source_ref, applied_ref, force_ref, image_ref, image2_ref, sums_ref,
    stress, src, force, image, kept,
):
    block = Block(own_ref.shape[1])
    block.clear_edges(stress, src, force, image)
    near = ((own_ref, first_ref, second_ref), (own_z_ref, None, None))

    def heated(side, layer, c, heat):
        s = block.masked(side, layer, JOULE_GAIN * (SIGMA_MIN + c) + heat)
        block.store(stress, side, layer, (MODULUS_MINIMUM + c) * s)
        return s

    for layer in range(1, 7):
        for side in range(2):
            for _ in block.strips():
                heat = block.read(heat_z_ref if side else heat_ref, layer - 1)
                s = heated(side, layer, block.load(cub, side, layer - 1), heat)
                if 2 <= layer <= 5:
                    block.store(src, side, layer - 2, s)
                if side == 0 and layer in (3, 4):
                    block.write(source_ref, s, layer - 3)
    for _ in block.strips():
        one, two = block.read(far_one_ref, 0), block.read(far_two_ref, 0)
        for layer, d in ((0, jnp.where(block.low_pair, two, one)), (7, jnp.where(block.low_pair, one, two))):
            heated(0, layer, d * d * d, block.read(heat_far_ref, layer // 7))
        for side, layer, index in ((0, 0, 1), (0, 2, 0), (1, 2, 0)):
            mirrored = jnp.where(
                block.gx == index, block.load(stress, side, layer + 1), block.load(stress, side, layer)
            )
            block.store(stress, side, layer, mirrored)

    half = EXPANSION * 0.5
    for layer in range(1, 7):
        for side in range(1 if layer in (1, 6) else 2):
            for _ in block.strips():
                _, down, up = block.z_pair(stress, layer, side)
                parts = (
                    block.load(stress, side, layer + 1) - block.load(stress, side, layer - 1),
                    block.load(stress, side, layer, 1) - block.load(stress, side, layer, -1),
                    up - down,
                )
                for k in range(3):
                    value = block.masked(side, layer, half * parts[k])
                    block.store(force, side, k * 6 + layer - 1, value)
                    if side == 0 and layer in (3, 4):
                        block.write(force_ref, value, k, layer - 3)

    for layer in range(2, 6):
        own = layer in (3, 4)
        for side in range(2 if own else 1):
            for _ in block.strips():
                weights = block.weights_of(cub, layer, side)
                anchor = PENALTY * block.pick(*near[side], layer, 4, 4)
                mine = own and side == 0
                for k in range(3):
                    v, parts = block.differences(force, k * 6 + layer - 1, side)
                    value = block.masked(side, layer, block.weighted(weights, parts) + anchor * v)
                    block.store(image, side, k * 4 + layer - 2, value)
                    if mine:
                        block.write(image_ref, value, k, layer - 3)
                        block.accumulate("n", v * v)
                        block.accumulate("m", v * value)
                if mine:
                    for k, weight in enumerate(weights):
                        block.write(kept, weight, layer - 3, k)
                    v, parts = block.differences(src, layer - 2, 0)
                    heat_weights = [w + SPREAD for w in weights]
                    if layer == 3:
                        heat_weights[0] = weights[0] + SPREAD * block.symmetry
                    heat_image = block.weighted(heat_weights, parts) + CONVECTION * v
                    block.write(applied_ref, heat_image, layer - 3)
                    block.accumulate("k", v * heat_image)
                    block.accumulate("q", v * v)
    n, m, k, q = (block.total(name) for name in "nmkq")
    theta = ratio(m, n)
    for layer in (3, 4):
        for _ in block.strips():
            weights = [block.read(kept, layer - 3, k6) for k6 in range(6)]
            anchor = PENALTY * block.read(own_ref, layer + 1)
            for k3 in range(3):
                v, parts = block.differences(image, k3 * 4 + layer - 2, 0)
                value = block.weighted(weights, parts) + anchor * v
                block.write(image2_ref, value, k3, layer - 3)
                start = block.load(force, 0, k3 * 6 + layer - 1)
                r = v - theta * start
                y = value - theta * v
                block.accumulate("s", r * r)
                block.accumulate("t", r * y)
                block.accumulate("c", start * y)
    s, t, c = (block.total(name) for name in "stc")
    row = row_ref[...] + block.row({0: q, 1: k, 4: n, 5: m, 6: s, 7: t, 8: c + s})
    sums_ref[...] = jnp.broadcast_to(row[None], sums_ref.shape)


def field(count, height):
    return (2, count, height + 2 * EDGE, WIDTH)


def in_memory(kernel, arguments, shapes, scratch):
    vmem = pl.BlockSpec(memory_space=pltpu.VMEM)
    return pl.pallas_call(
        kernel,
        out_shape=[jax.ShapeDtypeStruct(s, F32) for s in shapes],
        in_specs=[vmem] * len(arguments),
        out_specs=[vmem] * len(shapes),
        scratch_shapes=[pltpu.VMEM(s, F32) for s in scratch],
        compiler_params=pltpu.CompilerParams(vmem_limit_bytes=VMEM_LIMIT),
    )(*arguments)


def port_stage(arguments, layers, height):
    own = (layers, height, WIDTH)
    shapes = [field(6, height), own, own, own, (1, WIDTH)]
    return in_memory(port_kernel, arguments, shapes, [field(6, height), field(4, height), (2, 6, height, WIDTH)])


def force_stage(arguments, devices, layers, height):
    own = (layers, height, WIDTH)
    vectors = (3,) + own
    shapes = [own, own, vectors, vectors, vectors, (devices, 1, WIDTH)]
    scratch = [field(8, height), field(4, height), field(18, height), field(12, height), (2, 6, height, WIDTH)]
    return in_memory(force_kernel, arguments, shapes, scratch)


def final_kernel(
    table_ref, source_ref, own_ref, applied_ref, papplied_ref, force_ref, image_ref, image2_ref,
    pimage_ref, pimage2_ref,
    temperature_ref, adjoint_ref, displacement_ref, displacement_adjoint_ref, thermal_ref, elastic_ref,
):
    table = table_ref[...].reshape(table_ref.shape[0], WIDTH)

    def column(k):
        return table[:, k : k + 1]

    def total(value):
        return jnp.sum(value, axis=0, keepdims=True)

    step0 = total(column(0)) / total(column(1))
    step1 = total(column(2)) / total(column(3))

    def solve(first):
        n_all, m_all = column(first), column(first + 1)
        n, m = total(n_all), total(m_all)
        theta = m / n
        local = jnp.where(n_all > 0.0, m_all / jnp.where(n_all > 0.0, n_all, 1.0), 0.0)
        gap = local - theta
        s = total(column(first + 2) + gap * gap * n_all)
        t = total(column(first + 3) + gap * column(first + 4) + gap * gap * m_all)
        alpha0 = n / m
        beta = s * alpha0 * alpha0 / n
        alpha1 = s / (t - s * s / m)
        return alpha0, beta, alpha1

    def outcome(coefficients, b, w, u):
        alpha0, beta, alpha1 = coefficients
        r = b - alpha0 * w
        x = alpha0 * b + alpha1 * (r + beta * b)
        r = r - alpha1 * ((w - alpha0 * u) + beta * w)
        return x, r

    forward, adjoint = solve(4), solve(9)
    for layer in range(source_ref.shape[0]):
        source = source_ref[layer]
        port = own_ref[source_ref.shape[0] + layer]
        temperature_ref[layer] = step0 * source
        adjoint_ref[layer] = step1 * port
        thermal_ref[0, layer] = source - step0 * applied_ref[layer]
        thermal_ref[1, layer] = port - step1 * papplied_ref[layer]
        for k in range(3):
            x, r = outcome(forward, force_ref[k, layer], image_ref[k, layer], image2_ref[k, layer])
            displacement_ref[k, layer] = step0 * x
            elastic_ref[0, k, layer] = step0 * r
        x, r = outcome(adjoint, port, pimage_ref[layer], pimage2_ref[layer])
        for k in range(3):
            displacement_adjoint_ref[k, layer] = PORT_DIRECTION[k] * x
            elastic_ref[1, k, layer] = PORT_DIRECTION[k] * r


def final_stage(arguments, layers, height):
    own = (layers, height, WIDTH)
    shapes = [own, own, (3,) + own, (3,) + own, (2,) + own, (2, 3) + own]
    vmem = pl.BlockSpec(memory_space=pltpu.VMEM)
    return pl.pallas_call(
        final_kernel,
        out_shape=[jax.ShapeDtypeStruct(s, F32) for s in shapes],
        in_specs=[vmem] * len(arguments),
        out_specs=[vmem] * len(shapes),
        compiler_params=pltpu.CompilerParams(vmem_limit_bytes=VMEM_LIMIT),
        name="outputs",
    )(*arguments)


def per_device(density, anchor_mask, port_mask, heater_owner, heater_cell, heater_power):
    layers, height, _ = density.shape
    count = lax.axis_size("gx")
    devices = count * lax.axis_size("gz")
    heaters = tuple(a.reshape(1, -1) for a in (heater_owner, heater_cell, heater_power))
    heaters = tuple(pltpu.with_memory_space_constraint(a, pltpu.HBM) for a in (density, anchor_mask, port_mask) + heaters)
    first, second, far_one, far_two, own, entries = prepare(heaters, count)
    first = lax.ppermute(first, "gx", swap_pairs(count, 0, 1))
    second = lax.ppermute(second, "gx", swap_pairs(count, 1, 1))
    entries = lax.all_to_all(entries, "gx", 0, 0, tiled=True)
    far_one = lax.ppermute(far_one, "gx", swap_pairs(count, 0, 2))
    far_two = lax.ppermute(far_two, "gx", swap_pairs(count, 2, 2))
    own_z = across_z(own)
    first_z = across_z(first)
    second_z = across_z(second)
    heat, heat_far = scatter_heat(entries, layers, height)
    heat_z = across_z(heat)
    cub, papplied, pimage, pimage2, row = port_stage(
        (own, own_z, first, first_z, second, second_z), layers, height
    )
    source, applied, force, image, image2, sums = force_stage(
        (own, own_z, first, second, far_one, far_two, heat, heat_z, heat_far, cub, row), devices, layers, height
    )
    table = lax.all_to_all(sums, ("gx", "gz"), 0, 0, tiled=True)
    return tuple(
        final_stage(
            (table, source, own, applied, papplied, force, image, image2, pimage, pimage2), layers, height
        )
    )


def solution(mesh):
    in_specs = (
        P("gx", None, "gz"),
        P("gx", None, "gz"),
        P("gx", None, "gz"),
        P("gx", "gz", None, None),
        P("gx", "gz", None),
        P("gx", "gz", None),
    )
    out_specs = (
        P("gx", None, "gz"),
        P("gx", None, "gz"),
        P(None, "gx", None, "gz"),
        P(None, "gx", None, "gz"),
        P(None, "gx", None, "gz"),
        P(None, None, "gx", None, "gz"),
    )
    return jax.shard_map(per_device, mesh=mesh, in_specs=in_specs, out_specs=out_specs, check_vma=False)
```

```python
import functools

import jax
import jax.numpy as jnp
from jax import lax
from jax.experimental import pallas as pl
from jax.experimental.pallas import tpu as pltpu
from jax.sharding import PartitionSpec as P


KAPPA_MIN = 0.05
MODULUS_MINIMUM = 0.02
CONVECTION = 0.2
PENALTY = 10.0
JOULE_GAIN = 1.0
SIGMA_MIN = 0.1
EXPANSION = 4.0
PORT_DIRECTION = (1.0, 0.5, -0.5)


HALO = 3
WIDTH = 128
EDGE = 8
STRIP = 8
VMEM_LIMIT = 16 << 20
F32 = jnp.float32


def swap_pairs(count, offset, distance):
    pairs = []
    for low in range(offset, count - distance):
        if ((low - offset) // distance) % 2 == 0:
            pairs += [(low, low + distance), (low + distance, low)]
    return pairs


def across_z(values):
    count = lax.axis_size("gz")
    if count == 2:
        return lax.ppermute(values, "gz", [(0, 1), (1, 0)])
    upper = lax.ppermute(values, "gz", [(i + 1, i) for i in range(count - 1)])
    lower = lax.ppermute(values, "gz", [(i, i + 1) for i in range(count - 1)])
    lanes = lax.broadcasted_iota(jnp.int32, values.shape, values.ndim - 1)
    return jnp.where(lanes < WIDTH // 2, upper, lower)


def prepare_kernel(
    density_hbm, anchor_hbm, port_hbm, owner_hbm, cell_hbm, power_hbm,
    first_ref, second_ref, far_one_ref, far_two_ref, own_ref, entries_hbm,
    density_ref, anchor_ref, port_ref, owner_ref, cell_ref, power_ref, entries_ref, arrived,
):
    layers = density_ref.shape[0]
    sources = (owner_hbm, cell_hbm, power_hbm, density_hbm, port_hbm, anchor_hbm)
    targets = (owner_ref, cell_ref, power_ref, density_ref, port_ref, anchor_ref)
    copies = [
        pltpu.make_async_copy(source, target, arrived.at[k])
        for k, (source, target) in enumerate(zip(sources, targets))
    ]
    for copy in copies:
        copy.start()
    gx = lax.axis_index("gx")
    even = gx % 2 == 0
    low_pair = gx % 4 < 2
    for copy in copies[:3]:
        copy.wait()
    owner = owner_ref[...].astype(F32)
    cell = cell_ref[...].astype(F32)
    power = power_ref[...]
    for k in range(entries_ref.shape[0]):
        entries_ref[k, 0:1] = owner
        entries_ref[k, 1:2] = cell
        entries_ref[k, 2:3] = power
    leaving = pltpu.make_async_copy(entries_ref, entries_hbm, arrived.at[len(copies)])
    leaving.start()
    copies[3].wait()
    for layer in range(layers):
        density = density_ref[layer]
        for ref in (first_ref, second_ref, own_ref):
            ref[layer] = density
    below, above = density_ref[0], density_ref[layers - 1]
    far_one_ref[0] = jnp.where(low_pair, above, below)
    far_two_ref[0] = jnp.where(low_pair, below, above)
    copies[4].wait()
    for layer in range(layers):
        port = port_ref[layer].astype(F32)
        for ref in (first_ref, second_ref, own_ref):
            ref[layers + layer] = port
    copies[5].wait()
    for layer in range(layers):
        own_ref[2 * layers + layer] = anchor_ref[layer].astype(F32)
    below, above = anchor_ref[0].astype(F32), anchor_ref[layers - 1].astype(F32)
    first_ref[2 * layers] = jnp.where(even, above, below)
    second_ref[2 * layers] = jnp.where(even, below, above)
    leaving.wait()


def prepare(arguments, sources):
    layers, height, _ = arguments[0].shape
    plane = (height, WIDTH)
    shapes = [
        (2 * layers + 1,) + plane, (2 * layers + 1,) + plane, (1,) + plane, (1,) + plane,
        (3 * layers,) + plane, (sources, 3, arguments[-1].shape[1]),
    ]
    return pl.pallas_call(
        prepare_kernel,
        out_shape=[jax.ShapeDtypeStruct(s, F32) for s in shapes],
        in_specs=[pl.BlockSpec(memory_space=pltpu.HBM)] * len(arguments),
        out_specs=[pl.BlockSpec(memory_space=pltpu.VMEM)] * (len(shapes) - 1)
        + [pl.BlockSpec(memory_space=pltpu.HBM)],
        scratch_shapes=[pltpu.VMEM(a.shape, a.dtype) for a in arguments]
        + [pltpu.VMEM(shapes[-1], F32), pltpu.SemaphoreType.DMA((len(arguments) + 1,))],
        compiler_params=pltpu.CompilerParams(vmem_limit_bytes=VMEM_LIMIT),
        name="prepare",
    )(*arguments)


def heater_kernel(entries_ref, heat_ref, far_ref, rows_ref, lanes_ref, *total_refs, layers, height, block):
    sources = entries_ref.shape[0]
    entries = entries_ref.shape[2]
    slabs = layers + 2 * HALO
    base = lax.axis_index("gx") * layers - HALO
    plane_bits = (height * WIDTH).bit_length() - 1
    lane_bits = WIDTH.bit_length() - 1
    height_bits = height.bit_length() - 1
    group = slabs * height
    row_ids = lax.broadcasted_iota(jnp.int32, (group, entries), 0)
    lane_ids = lax.broadcasted_iota(jnp.int32, (WIDTH, entries), 0)

    def one_block(start, keep):
        rows = []
        for k in range(block):
            table = entries_ref[start + k]
            owner = table[0:1].astype(jnp.int32)
            cell = table[1:2].astype(jnp.int32)
            power = table[2:3]
            slab = owner * layers + (cell >> plane_bits) - base
            rows.append((slab << height_bits) + ((cell >> lane_bits) & (height - 1)))
            high = power.astype(jnp.bfloat16).astype(F32)
            low = power - high
            here = slice(k * entries, (k + 1) * entries)
            match = lane_ids == (cell & (WIDTH - 1))
            lanes_ref[0:WIDTH, here] = jnp.where(match, high, 0.0).astype(jnp.bfloat16)
            lanes_ref[WIDTH:, here] = jnp.where(match, low, 0.0).astype(jnp.bfloat16)
            rows_ref[:, here] = jnp.where(row_ids == rows[k], 1.0, 0.0).astype(jnp.bfloat16)
        both = None
        width = block * entries // 1
        for k in range(1):
            here = slice(k * width, (k + 1) * width)
            part = lax.dot_general(
                rows_ref[:, here], lanes_ref[:, here], (((1,), (1,)), ((), ())), preferred_element_type=F32
            )
            both = part if both is None else both + part
        keep(0, both[:, :WIDTH] + both[:, WIDTH:])

    def write(first, part):
        for k in range(group // height):
            slab = first // height + k
            value = part[k * height : (k + 1) * height]
            if slab in (0, slabs - 1):
                far_ref[slab // (slabs - 1)] = value
            else:
                heat_ref[slab - 1] = value

    if sources == block:
        one_block(0, write)
        return
    total_ref = total_refs[0]
    total_ref[...] = jnp.zeros_like(total_ref)

    def add(first, part):
        total_ref[first : first + group, :] += part

    @pl.loop(0, sources // block)
    def _(step):
        one_block(step * block, add)

    for first in range(0, slabs * height, group):
        write(first, total_ref[first : first + group, :])


def scatter_heat(entries, layers, height):
    sources, _, count = entries.shape
    block = min(sources, 16)
    slabs = layers + 2 * HALO
    if height & (height - 1) or sources % block:
        raise ValueError("unsupported sizes")
    scratch = [
        pltpu.VMEM((slabs * height, block * count), jnp.bfloat16),
        pltpu.VMEM((2 * WIDTH, block * count), jnp.bfloat16),
    ]
    if sources > block:
        scratch.append(pltpu.VMEM((slabs * height, WIDTH), F32))
    return pl.pallas_call(
        functools.partial(heater_kernel, layers=layers, height=height, block=block),
        out_shape=[jax.ShapeDtypeStruct((k, height, WIDTH), F32) for k in (slabs - 2, 2)],
        in_specs=[pl.BlockSpec(memory_space=pltpu.VMEM)],
        out_specs=[pl.BlockSpec(memory_space=pltpu.VMEM)] * 2,
        scratch_shapes=scratch,
        compiler_params=pltpu.CompilerParams(vmem_limit_bytes=VMEM_LIMIT),
        name="heater_scatter",
    )(entries)


class Block:
    def __init__(self, height):
        gx, gz = lax.axis_index("gx"), lax.axis_index("gz")
        last_x, last_z = lax.axis_size("gx") - 1, lax.axis_size("gz") - 1

        def flag(condition):
            return jnp.where(condition, 1.0, 0.0).astype(F32)

        self.gx = gx
        self.height = height
        self.start = 0
        self.even = gx % 2 == 0
        self.low_pair = gx % 4 < 2
        lanes = lax.broadcasted_iota(jnp.int32, (STRIP, WIDTH), 1)
        self.is_last = lanes == WIDTH - 1
        self.is_first = lanes == 0
        self.z_valid = jnp.where(lanes < WIDTH // 2, flag(gz < last_z), flag(gz > 0))
        self.x_valid = [
            flag(gx >= 2), flag(gx >= 1), flag(gx >= 1), None, None,
            flag(gx < last_x), flag(gx < last_x), flag(gx < last_x - 1),
        ]
        self.symmetry = flag(gx > 0)
        self.sums = {}

    def strips(self):
        for start in range(0, self.height, STRIP):
            self.start = start
            yield start

    def masked(self, side, layer, value):
        if side:
            value = value * self.z_valid
        if self.x_valid[layer] is not None:
            value = value * self.x_valid[layer]
        return value

    def load(self, ref, side, layer, shift=0):
        first = EDGE + self.start + shift
        return ref[side, layer, first : first + STRIP, :]

    def store(self, ref, side, layer, value):
        first = EDGE + self.start
        ref[side, layer, first : first + STRIP, :] = value

    def read(self, ref, *index):
        return ref[index + (slice(self.start, self.start + STRIP), slice(None))]

    def write(self, ref, value, *index):
        ref[index + (slice(self.start, self.start + STRIP), slice(None))] = value

    def clear_edges(self, *refs):
        edge_rows = jnp.zeros((EDGE, WIDTH), F32)
        for ref in refs:
            for side in range(2):
                for layer in range(ref.shape[1]):
                    ref[side, layer, 0:EDGE, :] = edge_rows
                    ref[side, layer, EDGE + self.height :, :] = edge_rows

    def z_pair(self, ref, layer, side):
        value, other = self.load(ref, side, layer), self.load(ref, 1 - side, layer)
        down = pltpu.roll(jnp.where(self.is_last, other, value), 1, 1)
        up = pltpu.roll(jnp.where(self.is_first, other, value), WIDTH - 1, 1)
        return value, down, up

    def pick(self, own, first, second, layer, own_tile, near_tile):
        if layer in (3, 4):
            return self.read(own, own_tile + layer - 3)
        one, two = (second, first) if layer < 3 else (first, second)
        return jnp.where(self.even, self.read(one, near_tile), self.read(two, near_tile))

    def weights_of(self, cub, layer, side):
        def face(a, b):
            return MODULUS_MINIMUM + 0.5 * (a + b)

        index = layer - 1
        c, down, up = self.z_pair(cub, index, side)
        x_low = face(self.load(cub, side, index - 1), c)
        if layer == 3:
            x_low = x_low * self.symmetry
        return (
            x_low,
            face(self.load(cub, side, index + 1), c),
            face(self.load(cub, side, index, -1), c),
            face(self.load(cub, side, index, 1), c),
            face(down, c),
            face(up, c),
        )

    def differences(self, ref, index, side):
        v, down, up = self.z_pair(ref, index, side)
        parts = (
            v - self.load(ref, side, index - 1),
            v - self.load(ref, side, index + 1),
            v - self.load(ref, side, index, -1),
            v - self.load(ref, side, index, 1),
            v - down,
            v - up,
        )
        return v, parts

    def weighted(self, weights, parts):
        total = weights[0] * parts[0]
        for w, p in zip(weights[1:], parts[1:]):
            total = total + w * p
        return total

    def accumulate(self, name, value):
        value = jnp.sum(value.reshape(STRIP // 8, 8, WIDTH), axis=0)
        self.sums[name] = self.sums[name] + value if name in self.sums else value

    def total(self, name):
        return jnp.sum(jnp.sum(self.sums[name], axis=0, keepdims=True), axis=1, keepdims=True)

    def row(self, columns):
        lane = lax.broadcasted_iota(jnp.int32, (1, WIDTH), 1)
        row = jnp.zeros((1, WIDTH), F32)
        for k, column in columns.items():
            row = jnp.where(lane == k, column, row)
        return row


def ratio(m, n):
    return jnp.where(n > 0.0, m / jnp.where(n > 0.0, n, 1.0), 0.0)


SPREAD = KAPPA_MIN - MODULUS_MINIMUM


def port_kernel(
    own_ref, own_z_ref, first_ref, first_z_ref, second_ref, second_z_ref,
    cub, applied_ref, image_ref, image2_ref, row_ref,
    prt, image, kept,
):
    block = Block(own_ref.shape[1])
    block.clear_edges(cub, prt, image)
    near = ((own_ref, first_ref, second_ref), (own_z_ref, first_z_ref, second_z_ref))
    for layer in range(1, 7):
        tile = (layer - 1) % 4
        for side in range(2):
            for _ in block.strips():
                d = block.masked(side, layer, block.pick(*near[side], layer, 0, tile))
                block.store(cub, side, layer - 1, d * d * d)
                if 2 <= layer <= 5 or side == 0:
                    port = block.masked(side, layer, block.pick(*near[side], layer, 2, 2 + tile))
                    block.store(prt, side, layer - 1, port)
    for layer in range(2, 6):
        own = layer in (3, 4)
        for side in range(2 if own else 1):
            for _ in block.strips():
                weights = block.weights_of(cub, layer, side)
                v, parts = block.differences(prt, layer - 1, side)
                flux = block.weighted(weights, parts)
                anchor = PENALTY * block.pick(*near[side], layer, 4, 4)
                value = block.masked(side, layer, flux + anchor * v)
                block.store(image, side, layer - 2, value)
                if own and side == 0:
                    for k, weight in enumerate(weights):
                        block.write(kept, weight, layer - 3, k)
                    block.write(image_ref, value, layer - 3)
                    block.accumulate("n", v * v)
                    block.accumulate("m", v * value)
                    low = parts[0] * block.symmetry if layer == 3 else parts[0]
                    plain = low + parts[1] + parts[2] + parts[3] + parts[4] + parts[5]
                    heat_image = flux + SPREAD * plain + CONVECTION * v
                    block.write(applied_ref, heat_image, layer - 3)
                    block.accumulate("k", v * heat_image)
    n, m, k = (block.total(name) for name in "nmk")
    theta = ratio(m, n)
    for layer in (3, 4):
        for _ in block.strips():
            v, parts = block.differences(image, layer - 2, 0)
            weights = [block.read(kept, layer - 3, k6) for k6 in range(6)]
            anchor = PENALTY * block.read(own_ref, layer + 1)
            value = block.weighted(weights, parts) + anchor * v
            block.write(image2_ref, value, layer - 3)
            start = block.load(prt, 0, layer - 1)
            r = v - theta * start
            y = value - theta * v
            block.accumulate("s", r * r)
            block.accumulate("t", r * y)
            block.accumulate("c", start * y)
    s, t, c = (block.total(name) for name in "stc")
    row_ref[...] = block.row({2: n, 3: k, 9: n, 10: m, 11: s, 12: t, 13: c + s})


def force_kernel(
    own_ref, own_z_ref, first_ref, second_ref, heat_ref, heat_z_ref, cub, partial_ref,
    source_ref, applied_ref, force_ref, image_ref, image2_ref, row_ref,
    stress, src, force, image, kept,
):
    block = Block(own_ref.shape[1])
    block.clear_edges(stress, src, force, image)
    near = ((own_ref, first_ref, second_ref), (own_z_ref, None, None))

    def heated(side, layer, c, heat):
        s = block.masked(side, layer, JOULE_GAIN * (SIGMA_MIN + c) + heat)
        block.store(stress, side, layer, (MODULUS_MINIMUM + c) * s)
        return s

    for layer in range(1, 7):
        for side in range(2):
            for _ in block.strips():
                heat = block.read(heat_z_ref if side else heat_ref, layer - 1)
                s = heated(side, layer, block.load(cub, side, layer - 1), heat)
                if 2 <= layer <= 5:
                    block.store(src, side, layer - 2, s)
                if side == 0 and layer in (3, 4):
                    block.write(source_ref, s, layer - 3)
    for _ in block.strips():
        zero = jnp.zeros((STRIP, WIDTH), F32)
        block.store(stress, 0, 0, jnp.where(block.gx == 1, block.load(stress, 0, 1), zero))
        block.store(stress, 0, 7, zero)
        for side in range(2):
            mirrored = jnp.where(block.gx == 0, block.load(stress, side, 3), block.load(stress, side, 2))
            block.store(stress, side, 2, mirrored)

    half = EXPANSION * 0.5
    for layer in range(1, 7):
        for side in range(1 if layer in (1, 6) else 2):
            for _ in block.strips():
                _, down, up = block.z_pair(stress, layer, side)
                parts = (
                    block.load(stress, side, layer + 1) - block.load(stress, side, layer - 1),
                    block.load(stress, side, layer, 1) - block.load(stress, side, layer, -1),
                    up - down,
                )
                for k in range(3):
                    value = block.masked(side, layer, half * parts[k])
                    block.store(force, side, k * 6 + layer - 1, value)
                    if side == 0 and layer in (3, 4):
                        block.write(force_ref, value, k, layer - 3)

    for layer in range(2, 6):
        own = layer in (3, 4)
        for side in range(2 if own else 1):
            for _ in block.strips():
                weights = block.weights_of(cub, layer, side)
                anchor = PENALTY * block.pick(*near[side], layer, 4, 4)
                mine = own and side == 0
                for k in range(3):
                    v, parts = block.differences(force, k * 6 + layer - 1, side)
                    value = block.masked(side, layer, block.weighted(weights, parts) + anchor * v)
                    block.store(image, side, k * 4 + layer - 2, value)
                    if mine:
                        block.write(image_ref, value, k, layer - 3)
                        block.accumulate("n", v * v)
                        block.accumulate("m", v * value)
                if mine:
                    for k, weight in enumerate(weights):
                        block.write(kept, weight, layer - 3, k)
                    v, parts = block.differences(src, layer - 2, 0)
                    heat_weights = [w + SPREAD for w in weights]
                    if layer == 3:
                        heat_weights[0] = weights[0] + SPREAD * block.symmetry
                    heat_image = block.weighted(heat_weights, parts) + CONVECTION * v
                    block.write(applied_ref, heat_image, layer - 3)
                    block.accumulate("k", v * heat_image)
                    block.accumulate("q", v * v)
    n, m, k, q = (block.total(name) for name in "nmkq")
    theta = ratio(m, n)
    for layer in (3, 4):
        for _ in block.strips():
            weights = [block.read(kept, layer - 3, k6) for k6 in range(6)]
            anchor = PENALTY * block.read(own_ref, layer + 1)
            for k3 in range(3):
                v, parts = block.differences(image, k3 * 4 + layer - 2, 0)
                value = block.weighted(weights, parts) + anchor * v
                block.write(image2_ref, value, k3, layer - 3)
                start = block.load(force, 0, k3 * 6 + layer - 1)
                r = v - theta * start
                y = value - theta * v
                block.accumulate("s", r * r)
                block.accumulate("t", r * y)
                block.accumulate("c", start * y)
    s, t, c = (block.total(name) for name in "stc")
    row_ref[...] = partial_ref[...] + block.row({0: q, 1: k, 4: n, 5: m, 6: s, 7: t, 8: c + s})


def far_kernel(
    far_one_ref, far_two_ref, heat_ref, cub, force_ref, image_ref, image2_ref, partial_ref,
    corrected_ref, sums_ref,
):
    block = Block(force_ref.shape[2])
    partial = partial_ref[...]
    theta = ratio(partial[:, 5:6], partial[:, 4:5])

    def face(a, b):
        return MODULUS_MINIMUM + 0.5 * (a + b)

    for _ in block.strips():
        one, two = block.read(far_one_ref, 0), block.read(far_two_ref, 0)
        for own, outer, d in (
            (0, 0, jnp.where(block.low_pair, two, one)),
            (1, 7, jnp.where(block.low_pair, one, two)),
        ):
            c = d * d * d
            stress = (MODULUS_MINIMUM + c) * (JOULE_GAIN * (SIGMA_MIN + c) + block.read(heat_ref, own))
            stress = block.masked(0, outer, stress)
            chain = [block.load(cub, 0, k) for k in ((0, 1, 2) if own == 0 else (5, 4, 3))]
            sign = -EXPANSION * 0.5 if own == 0 else EXPANSION * 0.5
            change = sign * face(chain[0], chain[1]) * face(chain[1], chain[2]) * stress
            block.write(corrected_ref, block.read(image2_ref, 0, own) + change, own)
            start = block.read(force_ref, 0, own)
            block.accumulate("t", (block.read(image_ref, 0, own) - theta * start) * change)
            block.accumulate("c", start * change)
    row = partial + block.row({7: block.total("t"), 8: block.total("c")})
    sums_ref[...] = jnp.broadcast_to(row[None], sums_ref.shape)


def field(count, height):
    return (2, count, height + 2 * EDGE, WIDTH)


def in_memory(kernel, arguments, shapes, scratch):
    vmem = pl.BlockSpec(memory_space=pltpu.VMEM)
    return pl.pallas_call(
        kernel,
        out_shape=[jax.ShapeDtypeStruct(s, F32) for s in shapes],
        in_specs=[vmem] * len(arguments),
        out_specs=[vmem] * len(shapes),
        scratch_shapes=[pltpu.VMEM(s, F32) for s in scratch],
        compiler_params=pltpu.CompilerParams(vmem_limit_bytes=VMEM_LIMIT),
    )(*arguments)


def port_stage(arguments, layers, height):
    own = (layers, height, WIDTH)
    shapes = [field(6, height), own, own, own, (1, WIDTH)]
    return in_memory(port_kernel, arguments, shapes, [field(6, height), field(4, height), (2, 6, height, WIDTH)])


def far_stage(arguments, devices, layers, height):
    return in_memory(far_kernel, arguments, [(layers, height, WIDTH), (devices, 1, WIDTH)], [])


def force_stage(arguments, layers, height):
    own = (layers, height, WIDTH)
    vectors = (3,) + own
    shapes = [own, own, vectors, vectors, vectors, (1, WIDTH)]
    scratch = [field(8, height), field(4, height), field(18, height), field(12, height), (2, 6, height, WIDTH)]
    return in_memory(force_kernel, arguments, shapes, scratch)


def final_kernel(
    table_ref, source_ref, own_ref, applied_ref, papplied_ref, force_ref, image_ref, image2_ref,
    corrected_ref, pimage_ref, pimage2_ref,
    temperature_ref, adjoint_ref, displacement_ref, displacement_adjoint_ref, thermal_ref, elastic_ref,
):
    table = table_ref[...].reshape(table_ref.shape[0], WIDTH)

    def column(k):
        return table[:, k : k + 1]

    def total(value):
        return jnp.sum(value, axis=0, keepdims=True)

    step0 = total(column(0)) / total(column(1))
    step1 = total(column(2)) / total(column(3))

    def solve(first):
        n_all, m_all = column(first), column(first + 1)
        n, m = total(n_all), total(m_all)
        theta = m / n
        local = jnp.where(n_all > 0.0, m_all / jnp.where(n_all > 0.0, n_all, 1.0), 0.0)
        gap = local - theta
        s = total(column(first + 2) + gap * gap * n_all)
        t = total(column(first + 3) + gap * column(first + 4) + gap * gap * m_all)
        alpha0 = n / m
        beta = s * alpha0 * alpha0 / n
        alpha1 = s / (t - s * s / m)
        return alpha0, beta, alpha1

    def outcome(coefficients, b, w, u):
        alpha0, beta, alpha1 = coefficients
        r = b - alpha0 * w
        x = alpha0 * b + alpha1 * (r + beta * b)
        r = r - alpha1 * ((w - alpha0 * u) + beta * w)
        return x, r

    forward, adjoint = solve(4), solve(9)
    for layer in range(source_ref.shape[0]):
        source = source_ref[layer]
        port = own_ref[source_ref.shape[0] + layer]
        temperature_ref[layer] = step0 * source
        adjoint_ref[layer] = step1 * port
        thermal_ref[0, layer] = source - step0 * applied_ref[layer]
        thermal_ref[1, layer] = port - step1 * papplied_ref[layer]
        for k in range(3):
            second = image2_ref[k, layer] if k else corrected_ref[layer]
            x, r = outcome(forward, force_ref[k, layer], image_ref[k, layer], second)
            displacement_ref[k, layer] = step0 * x
            elastic_ref[0, k, layer] = step0 * r
        x, r = outcome(adjoint, port, pimage_ref[layer], pimage2_ref[layer])
        for k in range(3):
            displacement_adjoint_ref[k, layer] = PORT_DIRECTION[k] * x
            elastic_ref[1, k, layer] = PORT_DIRECTION[k] * r


def final_stage(arguments, layers, height):
    own = (layers, height, WIDTH)
    shapes = [own, own, (3,) + own, (3,) + own, (2,) + own, (2, 3) + own]
    vmem = pl.BlockSpec(memory_space=pltpu.VMEM)
    return pl.pallas_call(
        final_kernel,
        out_shape=[jax.ShapeDtypeStruct(s, F32) for s in shapes],
        in_specs=[vmem] * len(arguments),
        out_specs=[vmem] * len(shapes),
        compiler_params=pltpu.CompilerParams(vmem_limit_bytes=VMEM_LIMIT),
        name="outputs",
    )(*arguments)


def per_device(density, anchor_mask, port_mask, heater_owner, heater_cell, heater_power):
    layers, height, _ = density.shape
    count = lax.axis_size("gx")
    devices = count * lax.axis_size("gz")
    heaters = tuple(a.reshape(1, -1) for a in (heater_owner, heater_cell, heater_power))
    heaters = tuple(pltpu.with_memory_space_constraint(a, pltpu.HBM) for a in (density, anchor_mask, port_mask) + heaters)
    first, second, far_one, far_two, own, entries = prepare(heaters, count)
    first = lax.ppermute(first, "gx", swap_pairs(count, 0, 1))
    second = lax.ppermute(second, "gx", swap_pairs(count, 1, 1))
    entries = lax.all_to_all(entries, "gx", 0, 0, tiled=True)
    far_one = lax.ppermute(far_one, "gx", swap_pairs(count, 0, 2))
    far_two = lax.ppermute(far_two, "gx", swap_pairs(count, 2, 2))
    own_z = across_z(own)
    first_z = across_z(first)
    second_z = across_z(second)
    heat, heat_far = scatter_heat(entries, layers, height)
    heat_z = across_z(heat)
    cub, papplied, pimage, pimage2, row = port_stage(
        (own, own_z, first, first_z, second, second_z), layers, height
    )
    source, applied, force, image, image2, row = force_stage(
        (own, own_z, first, second, heat, heat_z, cub, row), layers, height
    )
    corrected, sums = far_stage(
        (far_one, far_two, heat_far, cub, force, image, image2, row), devices, layers, height
    )
    table = lax.all_to_all(sums, ("gx", "gz"), 0, 0, tiled=True)
    return tuple(
        final_stage(
            (table, source, own, applied, papplied, force, image, image2, corrected, pimage, pimage2), layers, height
        )
    )


def solution(mesh):
    in_specs = (
        P("gx", None, "gz"),
        P("gx", None, "gz"),
        P("gx", None, "gz"),
        P("gx", "gz", None, None),
        P("gx", "gz", None),
        P("gx", "gz", None),
    )
    out_specs = (
        P("gx", None, "gz"),
        P("gx", None, "gz"),
        P(None, "gx", None, "gz"),
        P(None, "gx", None, "gz"),
        P(None, "gx", None, "gz"),
        P(None, None, "gx", None, "gz"),
    )
    return jax.shard_map(per_device, mesh=mesh, in_specs=in_specs, out_specs=out_specs, check_vma=False)
```

```python
import functools

import jax
import jax.numpy as jnp
from jax import lax
from jax.experimental import pallas as pl
from jax.experimental.pallas import tpu as pltpu
from jax.sharding import PartitionSpec as P


KAPPA_MIN = 0.05
MODULUS_MINIMUM = 0.02
CONVECTION = 0.2
PENALTY = 10.0
JOULE_GAIN = 1.0
SIGMA_MIN = 0.1
EXPANSION = 4.0
PORT_DIRECTION = (1.0, 0.5, -0.5)


HALO = 3
WIDTH = 128
EDGE = 8
STRIP = 8
VMEM_LIMIT = 16 << 20
F32 = jnp.float32


def swap_pairs(count, offset, distance):
    pairs = []
    for low in range(offset, count - distance):
        if ((low - offset) // distance) % 2 == 0:
            pairs += [(low, low + distance), (low + distance, low)]
    return pairs


def across_z(values):
    count = lax.axis_size("gz")
    if count == 2:
        return lax.ppermute(values, "gz", [(0, 1), (1, 0)])
    upper = lax.ppermute(values, "gz", [(i + 1, i) for i in range(count - 1)])
    lower = lax.ppermute(values, "gz", [(i, i + 1) for i in range(count - 1)])
    lanes = lax.broadcasted_iota(jnp.int32, values.shape, values.ndim - 1)
    return jnp.where(lanes < WIDTH // 2, upper, lower)


def prepare_kernel(
    density_hbm, anchor_hbm, port_hbm, owner_hbm, cell_hbm, power_hbm,
    first_ref, second_ref, far_one_ref, far_two_ref, own_ref, entries_hbm,
    density_ref, anchor_ref, port_ref, owner_ref, cell_ref, power_ref, entries_ref, arrived,
):
    layers = density_ref.shape[0]
    sources = (owner_hbm, cell_hbm, power_hbm, density_hbm, port_hbm, anchor_hbm)
    targets = (owner_ref, cell_ref, power_ref, density_ref, port_ref, anchor_ref)
    copies = [
        pltpu.make_async_copy(source, target, arrived.at[k])
        for k, (source, target) in enumerate(zip(sources, targets))
    ]
    for copy in copies:
        copy.start()
    gx = lax.axis_index("gx")
    even = gx % 2 == 0
    low_pair = gx % 4 < 2
    for copy in copies[:3]:
        copy.wait()
    owner = owner_ref[...].astype(F32)
    cell = cell_ref[...].astype(F32)
    power = power_ref[...]
    for k in range(entries_ref.shape[0]):
        entries_ref[k, 0:1] = owner
        entries_ref[k, 1:2] = cell
        entries_ref[k, 2:3] = power
    leaving = pltpu.make_async_copy(entries_ref, entries_hbm, arrived.at[len(copies)])
    leaving.start()
    copies[3].wait()
    for layer in range(layers):
        density = density_ref[layer]
        for ref in (first_ref, second_ref, own_ref):
            ref[layer] = density
    below, above = density_ref[0], density_ref[layers - 1]
    far_one_ref[0] = jnp.where(low_pair, above, below)
    far_two_ref[0] = jnp.where(low_pair, below, above)
    copies[4].wait()
    for layer in range(layers):
        port = port_ref[layer].astype(F32)
        for ref in (first_ref, second_ref, own_ref):
            ref[layers + layer] = port
    copies[5].wait()
    for layer in range(layers):
        own_ref[2 * layers + layer] = anchor_ref[layer].astype(F32)
    below, above = anchor_ref[0].astype(F32), anchor_ref[layers - 1].astype(F32)
    first_ref[2 * layers] = jnp.where(even, above, below)
    second_ref[2 * layers] = jnp.where(even, below, above)
    leaving.wait()


def prepare(arguments, sources):
    layers, height, _ = arguments[0].shape
    plane = (height, WIDTH)
    shapes = [
        (2 * layers + 1,) + plane, (2 * layers + 1,) + plane, (1,) + plane, (1,) + plane,
        (3 * layers,) + plane, (sources, 3, arguments[-1].shape[1]),
    ]
    return pl.pallas_call(
        prepare_kernel,
        out_shape=[jax.ShapeDtypeStruct(s, F32) for s in shapes],
        in_specs=[pl.BlockSpec(memory_space=pltpu.HBM)] * len(arguments),
        out_specs=[pl.BlockSpec(memory_space=pltpu.VMEM)] * (len(shapes) - 1)
        + [pl.BlockSpec(memory_space=pltpu.HBM)],
        scratch_shapes=[pltpu.VMEM(a.shape, a.dtype) for a in arguments]
        + [pltpu.VMEM(shapes[-1], F32), pltpu.SemaphoreType.DMA((len(arguments) + 1,))],
        compiler_params=pltpu.CompilerParams(vmem_limit_bytes=VMEM_LIMIT),
        name="prepare",
    )(*arguments)


def heater_kernel(entries_ref, heat_ref, rows_ref, lanes_ref, *total_refs, layers, block, outermost):
    sources = entries_ref.shape[0]
    entries = entries_ref.shape[2]
    slabs, height, _ = heat_ref.shape
    base = lax.axis_index("gx") * layers - HALO
    last = layers + 2 * HALO - 1
    plane_bits = (height * WIDTH).bit_length() - 1
    lane_bits = WIDTH.bit_length() - 1
    height_bits = height.bit_length() - 1
    row_ids = lax.broadcasted_iota(jnp.int32, (slabs * height, entries), 0)
    lane_ids = lax.broadcasted_iota(jnp.int32, (WIDTH, entries), 0)

    def one_block(start):
        for k in range(block):
            table = entries_ref[start + k]
            owner = table[0:1].astype(jnp.int32)
            cell = table[1:2].astype(jnp.int32)
            power = table[2:3]
            slab = owner * layers + (cell >> plane_bits) - base
            if outermost:
                place = jnp.where(slab == 0, 0, jnp.where(slab == last, 1, -1))
            else:
                place = slab - 1
            row = (place << height_bits) + ((cell >> lane_bits) & (height - 1))
            high = power.astype(jnp.bfloat16).astype(F32)
            low = power - high
            here = slice(k * entries, (k + 1) * entries)
            match = lane_ids == (cell & (WIDTH - 1))
            lanes_ref[0:WIDTH, here] = jnp.where(match, high, 0.0).astype(jnp.bfloat16)
            lanes_ref[WIDTH:, here] = jnp.where(match, low, 0.0).astype(jnp.bfloat16)
            rows_ref[:, here] = jnp.where(row_ids == row, 1.0, 0.0).astype(jnp.bfloat16)
        both = lax.dot_general(
            rows_ref[...], lanes_ref[...], (((1,), (1,)), ((), ())), preferred_element_type=F32
        )
        return both[:, :WIDTH] + both[:, WIDTH:]

    if sources == block:
        total = one_block(0)
    else:
        total_ref = total_refs[0]
        total_ref[...] = jnp.zeros_like(total_ref)

        @pl.loop(0, sources // block)
        def _(step):
            total_ref[...] += one_block(step * block)

        total = total_ref[...]
    heat_ref[...] = total.reshape(slabs, height, WIDTH)


def scatter_heat(entries, layers, height, outermost):
    sources, _, count = entries.shape
    block = min(sources, 16)
    slabs = 2 if outermost else layers + 2 * HALO - 2
    if height & (height - 1) or sources % block:
        raise ValueError("unsupported sizes")
    scratch = [
        pltpu.VMEM((slabs * height, block * count), jnp.bfloat16),
        pltpu.VMEM((2 * WIDTH, block * count), jnp.bfloat16),
    ]
    if sources > block:
        scratch.append(pltpu.VMEM((slabs * height, WIDTH), F32))
    return pl.pallas_call(
        functools.partial(heater_kernel, layers=layers, block=block, outermost=outermost),
        out_shape=jax.ShapeDtypeStruct((slabs, height, WIDTH), F32),
        in_specs=[pl.BlockSpec(memory_space=pltpu.VMEM)],
        out_specs=pl.BlockSpec(memory_space=pltpu.VMEM),
        scratch_shapes=scratch,
        compiler_params=pltpu.CompilerParams(vmem_limit_bytes=VMEM_LIMIT),
        name="far_scatter" if outermost else "heater_scatter",
    )(entries)


class Block:
    def __init__(self, height):
        gx, gz = lax.axis_index("gx"), lax.axis_index("gz")
        last_x, last_z = lax.axis_size("gx") - 1, lax.axis_size("gz") - 1

        def flag(condition):
            return jnp.where(condition, 1.0, 0.0).astype(F32)

        self.gx = gx
        self.height = height
        self.start = 0
        self.even = gx % 2 == 0
        self.low_pair = gx % 4 < 2
        lanes = lax.broadcasted_iota(jnp.int32, (STRIP, WIDTH), 1)
        self.is_last = lanes == WIDTH - 1
        self.is_first = lanes == 0
        self.z_valid = jnp.where(lanes < WIDTH // 2, flag(gz < last_z), flag(gz > 0))
        self.x_valid = [
            flag(gx >= 2), flag(gx >= 1), flag(gx >= 1), None, None,
            flag(gx < last_x), flag(gx < last_x), flag(gx < last_x - 1),
        ]
        self.symmetry = flag(gx > 0)
        self.sums = {}

    def strips(self):
        for start in range(0, self.height, STRIP):
            self.start = start
            yield start

    def masked(self, side, layer, value):
        if side:
            value = value * self.z_valid
        if self.x_valid[layer] is not None:
            value = value * self.x_valid[layer]
        return value

    def load(self, ref, side, layer, shift=0):
        first = EDGE + self.start + shift
        return ref[side, layer, first : first + STRIP, :]

    def store(self, ref, side, layer, value):
        first = EDGE + self.start
        ref[side, layer, first : first + STRIP, :] = value

    def read(self, ref, *index):
        return ref[index + (slice(self.start, self.start + STRIP), slice(None))]

    def write(self, ref, value, *index):
        ref[index + (slice(self.start, self.start + STRIP), slice(None))] = value

    def clear_edges(self, *refs):
        edge_rows = jnp.zeros((EDGE, WIDTH), F32)
        for ref in refs:
            for side in range(2):
                for layer in range(ref.shape[1]):
                    ref[side, layer, 0:EDGE, :] = edge_rows
                    ref[side, layer, EDGE + self.height :, :] = edge_rows

    def z_pair(self, ref, layer, side):
        value, other = self.load(ref, side, layer), self.load(ref, 1 - side, layer)
        down = pltpu.roll(jnp.where(self.is_last, other, value), 1, 1)
        up = pltpu.roll(jnp.where(self.is_first, other, value), WIDTH - 1, 1)
        return value, down, up

    def pick(self, own, first, second, layer, own_tile, near_tile):
        if layer in (3, 4):
            return self.read(own, own_tile + layer - 3)
        one, two = (second, first) if layer < 3 else (first, second)
        return jnp.where(self.even, self.read(one, near_tile), self.read(two, near_tile))

    def weights_of(self, cub, layer, side):
        def face(a, b):
            return MODULUS_MINIMUM + 0.5 * (a + b)

        index = layer - 1
        c, down, up = self.z_pair(cub, index, side)
        x_low = face(self.load(cub, side, index - 1), c)
        if layer == 3:
            x_low = x_low * self.symmetry
        return (
            x_low,
            face(self.load(cub, side, index + 1), c),
            face(self.load(cub, side, index, -1), c),
            face(self.load(cub, side, index, 1), c),
            face(down, c),
            face(up, c),
        )

    def differences(self, ref, index, side):
        v, down, up = self.z_pair(ref, index, side)
        parts = (
            v - self.load(ref, side, index - 1),
            v - self.load(ref, side, index + 1),
            v - self.load(ref, side, index, -1),
            v - self.load(ref, side, index, 1),
            v - down,
            v - up,
        )
        return v, parts

    def weighted(self, weights, parts):
        total = weights[0] * parts[0]
        for w, p in zip(weights[1:], parts[1:]):
            total = total + w * p
        return total

    def accumulate(self, name, value):
        value = jnp.sum(value.reshape(STRIP // 8, 8, WIDTH), axis=0)
        self.sums[name] = self.sums[name] + value if name in self.sums else value

    def total(self, name):
        return jnp.sum(jnp.sum(self.sums[name], axis=0, keepdims=True), axis=1, keepdims=True)

    def row(self, columns):
        lane = lax.broadcasted_iota(jnp.int32, (1, WIDTH), 1)
        row = jnp.zeros((1, WIDTH), F32)
        for k, column in columns.items():
            row = jnp.where(lane == k, column, row)
        return row


def ratio(m, n):
    return jnp.where(n > 0.0, m / jnp.where(n > 0.0, n, 1.0), 0.0)


SPREAD = KAPPA_MIN - MODULUS_MINIMUM


def port_kernel(
    own_ref, own_z_ref, first_ref, first_z_ref, second_ref, second_z_ref,
    cub, applied_ref, image_ref, image2_ref, row_ref,
    prt, image, kept,
):
    block = Block(own_ref.shape[1])
    block.clear_edges(cub, prt, image)
    near = ((own_ref, first_ref, second_ref), (own_z_ref, first_z_ref, second_z_ref))
    for layer in range(1, 7):
        tile = (layer - 1) % 4
        for side in range(2):
            for _ in block.strips():
                d = block.masked(side, layer, block.pick(*near[side], layer, 0, tile))
                block.store(cub, side, layer - 1, d * d * d)
                if 2 <= layer <= 5 or side == 0:
                    port = block.masked(side, layer, block.pick(*near[side], layer, 2, 2 + tile))
                    block.store(prt, side, layer - 1, port)
    for layer in range(2, 6):
        own = layer in (3, 4)
        for side in range(2 if own else 1):
            for _ in block.strips():
                weights = block.weights_of(cub, layer, side)
                v, parts = block.differences(prt, layer - 1, side)
                flux = block.weighted(weights, parts)
                anchor = PENALTY * block.pick(*near[side], layer, 4, 4)
                value = block.masked(side, layer, flux + anchor * v)
                block.store(image, side, layer - 2, value)
                if own and side == 0:
                    for k, weight in enumerate(weights):
                        block.write(kept, weight, layer - 3, k)
                    block.write(image_ref, value, layer - 3)
                    block.accumulate("n", v * v)
                    block.accumulate("m", v * value)
                    low = parts[0] * block.symmetry if layer == 3 else parts[0]
                    plain = low + parts[1] + parts[2] + parts[3] + parts[4] + parts[5]
                    heat_image = flux + SPREAD * plain + CONVECTION * v
                    block.write(applied_ref, heat_image, layer - 3)
                    block.accumulate("k", v * heat_image)
    n, m, k = (block.total(name) for name in "nmk")
    theta = ratio(m, n)
    for layer in (3, 4):
        for _ in block.strips():
            v, parts = block.differences(image, layer - 2, 0)
            weights = [block.read(kept, layer - 3, k6) for k6 in range(6)]
            anchor = PENALTY * block.read(own_ref, layer + 1)
            value = block.weighted(weights, parts) + anchor * v
            block.write(image2_ref, value, layer - 3)
            start = block.load(prt, 0, layer - 1)
            r = v - theta * start
            y = value - theta * v
            block.accumulate("s", r * r)
            block.accumulate("t", r * y)
            block.accumulate("c", start * y)
    s, t, c = (block.total(name) for name in "stc")
    row_ref[...] = block.row({2: n, 3: k, 9: n, 10: m, 11: s, 12: t, 13: c + s})


def force_kernel(
    own_ref, own_z_ref, first_ref, second_ref, heat_ref, heat_z_ref, cub, partial_ref,
    source_ref, applied_ref, force_ref, image_ref, image2_ref, row_ref,
    stress, src, force, image, kept,
):
    block = Block(own_ref.shape[1])
    block.clear_edges(stress, src, force, image)
    near = ((own_ref, first_ref, second_ref), (own_z_ref, None, None))

    def heated(side, layer, c, heat):
        s = block.masked(side, layer, JOULE_GAIN * (SIGMA_MIN + c) + heat)
        block.store(stress, side, layer, (MODULUS_MINIMUM + c) * s)
        return s

    for layer in range(1, 7):
        for side in range(2):
            for _ in block.strips():
                heat = block.read(heat_z_ref if side else heat_ref, layer - 1)
                s = heated(side, layer, block.load(cub, side, layer - 1), heat)
                if 2 <= layer <= 5:
                    block.store(src, side, layer - 2, s)
                if side == 0 and layer in (3, 4):
                    block.write(source_ref, s, layer - 3)
    for _ in block.strips():
        zero = jnp.zeros((STRIP, WIDTH), F32)
        block.store(stress, 0, 0, jnp.where(block.gx == 1, block.load(stress, 0, 1), zero))
        block.store(stress, 0, 7, zero)
        for side in range(2):
            mirrored = jnp.where(block.gx == 0, block.load(stress, side, 3), block.load(stress, side, 2))
            block.store(stress, side, 2, mirrored)

    half = EXPANSION * 0.5
    for layer in range(1, 7):
        for side in range(1 if layer in (1, 6) else 2):
            for _ in block.strips():
                _, down, up = block.z_pair(stress, layer, side)
                parts = (
                    block.load(stress, side, layer + 1) - block.load(stress, side, layer - 1),
                    block.load(stress, side, layer, 1) - block.load(stress, side, layer, -1),
                    up - down,
                )
                for k in range(3):
                    value = block.masked(side, layer, half * parts[k])
                    block.store(force, side, k * 6 + layer - 1, value)
                    if side == 0 and layer in (3, 4):
                        block.write(force_ref, value, k, layer - 3)

    for layer in range(2, 6):
        own = layer in (3, 4)
        for side in range(2 if own else 1):
            for _ in block.strips():
                weights = block.weights_of(cub, layer, side)
                anchor = PENALTY * block.pick(*near[side], layer, 4, 4)
                mine = own and side == 0
                for k in range(3):
                    v, parts = block.differences(force, k * 6 + layer - 1, side)
                    value = block.masked(side, layer, block.weighted(weights, parts) + anchor * v)
                    block.store(image, side, k * 4 + layer - 2, value)
                    if mine:
                        block.write(image_ref, value, k, layer - 3)
                        block.accumulate("n", v * v)
                        block.accumulate("m", v * value)
                if mine:
                    for k, weight in enumerate(weights):
                        block.write(kept, weight, layer - 3, k)
                    v, parts = block.differences(src, layer - 2, 0)
                    heat_weights = [w + SPREAD for w in weights]
                    if layer == 3:
                        heat_weights[0] = weights[0] + SPREAD * block.symmetry
                    heat_image = block.weighted(heat_weights, parts) + CONVECTION * v
                    block.write(applied_ref, heat_image, layer - 3)
                    block.accumulate("k", v * heat_image)
                    block.accumulate("q", v * v)
    n, m, k, q = (block.total(name) for name in "nmkq")
    theta = ratio(m, n)
    for layer in (3, 4):
        for _ in block.strips():
            weights = [block.read(kept, layer - 3, k6) for k6 in range(6)]
            anchor = PENALTY * block.read(own_ref, layer + 1)
            for k3 in range(3):
                v, parts = block.differences(image, k3 * 4 + layer - 2, 0)
                value = block.weighted(weights, parts) + anchor * v
                block.write(image2_ref, value, k3, layer - 3)
                start = block.load(force, 0, k3 * 6 + layer - 1)
                r = v - theta * start
                y = value - theta * v
                block.accumulate("s", r * r)
                block.accumulate("t", r * y)
                block.accumulate("c", start * y)
    s, t, c = (block.total(name) for name in "stc")
    row_ref[...] = partial_ref[...] + block.row({0: q, 1: k, 4: n, 5: m, 6: s, 7: t, 8: c + s})


def far_kernel(
    far_one_ref, far_two_ref, heat_ref, cub, force_ref, image_ref, image2_ref, partial_ref,
    corrected_ref, sums_ref,
):
    block = Block(force_ref.shape[2])
    partial = partial_ref[...]
    theta = ratio(partial[:, 5:6], partial[:, 4:5])

    def face(a, b):
        return MODULUS_MINIMUM + 0.5 * (a + b)

    for _ in block.strips():
        one, two = block.read(far_one_ref, 0), block.read(far_two_ref, 0)
        for own, outer, d in (
            (0, 0, jnp.where(block.low_pair, two, one)),
            (1, 7, jnp.where(block.low_pair, one, two)),
        ):
            c = d * d * d
            stress = (MODULUS_MINIMUM + c) * (JOULE_GAIN * (SIGMA_MIN + c) + block.read(heat_ref, own))
            stress = block.masked(0, outer, stress)
            chain = [block.load(cub, 0, k) for k in ((0, 1, 2) if own == 0 else (5, 4, 3))]
            sign = -EXPANSION * 0.5 if own == 0 else EXPANSION * 0.5
            change = sign * face(chain[0], chain[1]) * face(chain[1], chain[2]) * stress
            block.write(corrected_ref, block.read(image2_ref, 0, own) + change, own)
            start = block.read(force_ref, 0, own)
            block.accumulate("t", (block.read(image_ref, 0, own) - theta * start) * change)
            block.accumulate("c", start * change)
    row = partial + block.row({7: block.total("t"), 8: block.total("c")})
    sums_ref[...] = jnp.broadcast_to(row[None], sums_ref.shape)


def field(count, height):
    return (2, count, height + 2 * EDGE, WIDTH)


def in_memory(kernel, arguments, shapes, scratch):
    vmem = pl.BlockSpec(memory_space=pltpu.VMEM)
    return pl.pallas_call(
        kernel,
        out_shape=[jax.ShapeDtypeStruct(s, F32) for s in shapes],
        in_specs=[vmem] * len(arguments),
        out_specs=[vmem] * len(shapes),
        scratch_shapes=[pltpu.VMEM(s, F32) for s in scratch],
        compiler_params=pltpu.CompilerParams(vmem_limit_bytes=VMEM_LIMIT),
    )(*arguments)


def port_stage(arguments, layers, height):
    own = (layers, height, WIDTH)
    shapes = [field(6, height), own, own, own, (1, WIDTH)]
    return in_memory(port_kernel, arguments, shapes, [field(6, height), field(4, height), (2, 6, height, WIDTH)])


def far_stage(arguments, devices, layers, height):
    return in_memory(far_kernel, arguments, [(layers, height, WIDTH), (devices, 1, WIDTH)], [])


def force_stage(arguments, layers, height):
    own = (layers, height, WIDTH)
    vectors = (3,) + own
    shapes = [own, own, vectors, vectors, vectors, (1, WIDTH)]
    scratch = [field(8, height), field(4, height), field(18, height), field(12, height), (2, 6, height, WIDTH)]
    return in_memory(force_kernel, arguments, shapes, scratch)


def final_kernel(
    table_ref, source_ref, own_ref, applied_ref, papplied_ref, force_ref, image_ref, image2_ref,
    corrected_ref, pimage_ref, pimage2_ref,
    temperature_ref, adjoint_ref, displacement_ref, displacement_adjoint_ref, thermal_ref, elastic_ref,
):
    table = table_ref[...].reshape(table_ref.shape[0], WIDTH)

    def column(k):
        return table[:, k : k + 1]

    def total(value):
        return jnp.sum(value, axis=0, keepdims=True)

    step0 = total(column(0)) / total(column(1))
    step1 = total(column(2)) / total(column(3))

    def solve(first):
        n_all, m_all = column(first), column(first + 1)
        n, m = total(n_all), total(m_all)
        theta = m / n
        local = jnp.where(n_all > 0.0, m_all / jnp.where(n_all > 0.0, n_all, 1.0), 0.0)
        gap = local - theta
        s = total(column(first + 2) + gap * gap * n_all)
        t = total(column(first + 3) + gap * column(first + 4) + gap * gap * m_all)
        alpha0 = n / m
        beta = s * alpha0 * alpha0 / n
        alpha1 = s / (t - s * s / m)
        return alpha0, beta, alpha1

    def outcome(coefficients, b, w, u):
        alpha0, beta, alpha1 = coefficients
        r = b - alpha0 * w
        x = alpha0 * b + alpha1 * (r + beta * b)
        r = r - alpha1 * ((w - alpha0 * u) + beta * w)
        return x, r

    forward, adjoint = solve(4), solve(9)
    for layer in range(source_ref.shape[0]):
        source = source_ref[layer]
        port = own_ref[source_ref.shape[0] + layer]
        temperature_ref[layer] = step0 * source
        adjoint_ref[layer] = step1 * port
        thermal_ref[0, layer] = source - step0 * applied_ref[layer]
        thermal_ref[1, layer] = port - step1 * papplied_ref[layer]
        for k in range(3):
            second = image2_ref[k, layer] if k else corrected_ref[layer]
            x, r = outcome(forward, force_ref[k, layer], image_ref[k, layer], second)
            displacement_ref[k, layer] = step0 * x
            elastic_ref[0, k, layer] = step0 * r
        x, r = outcome(adjoint, port, pimage_ref[layer], pimage2_ref[layer])
        for k in range(3):
            displacement_adjoint_ref[k, layer] = PORT_DIRECTION[k] * x
            elastic_ref[1, k, layer] = PORT_DIRECTION[k] * r


def final_stage(arguments, layers, height):
    own = (layers, height, WIDTH)
    shapes = [own, own, (3,) + own, (3,) + own, (2,) + own, (2, 3) + own]
    vmem = pl.BlockSpec(memory_space=pltpu.VMEM)
    return pl.pallas_call(
        final_kernel,
        out_shape=[jax.ShapeDtypeStruct(s, F32) for s in shapes],
        in_specs=[vmem] * len(arguments),
        out_specs=[vmem] * len(shapes),
        compiler_params=pltpu.CompilerParams(vmem_limit_bytes=VMEM_LIMIT),
        name="outputs",
    )(*arguments)


def per_device(density, anchor_mask, port_mask, heater_owner, heater_cell, heater_power):
    layers, height, _ = density.shape
    count = lax.axis_size("gx")
    devices = count * lax.axis_size("gz")
    heaters = tuple(a.reshape(1, -1) for a in (heater_owner, heater_cell, heater_power))
    heaters = tuple(pltpu.with_memory_space_constraint(a, pltpu.HBM) for a in (density, anchor_mask, port_mask) + heaters)
    first, second, far_one, far_two, own, entries = prepare(heaters, count)
    first = lax.ppermute(first, "gx", swap_pairs(count, 0, 1))
    second = lax.ppermute(second, "gx", swap_pairs(count, 1, 1))
    entries = lax.all_to_all(entries, "gx", 0, 0, tiled=True)
    far_one = lax.ppermute(far_one, "gx", swap_pairs(count, 0, 2))
    far_two = lax.ppermute(far_two, "gx", swap_pairs(count, 2, 2))
    own_z = across_z(own)
    first_z = across_z(first)
    second_z = across_z(second)
    heat = scatter_heat(entries, layers, height, False)
    heat_far = scatter_heat(entries, layers, height, True)
    heat_z = across_z(heat)
    cub, papplied, pimage, pimage2, row = port_stage(
        (own, own_z, first, first_z, second, second_z), layers, height
    )
    source, applied, force, image, image2, row = force_stage(
        (own, own_z, first, second, heat, heat_z, cub, row), layers, height
    )
    corrected, sums = far_stage(
        (far_one, far_two, heat_far, cub, force, image, image2, row), devices, layers, height
    )
    table = lax.all_to_all(sums, ("gx", "gz"), 0, 0, tiled=True)
    return tuple(
        final_stage(
            (table, source, own, applied, papplied, force, image, image2, corrected, pimage, pimage2), layers, height
        )
    )


def solution(mesh):
    in_specs = (
        P("gx", None, "gz"),
        P("gx", None, "gz"),
        P("gx", None, "gz"),
        P("gx", "gz", None, None),
        P("gx", "gz", None),
        P("gx", "gz", None),
    )
    out_specs = (
        P("gx", None, "gz"),
        P("gx", None, "gz"),
        P(None, "gx", None, "gz"),
        P(None, "gx", None, "gz"),
        P(None, "gx", None, "gz"),
        P(None, None, "gx", None, "gz"),
    )
    return jax.shard_map(per_device, mesh=mesh, in_specs=in_specs, out_specs=out_specs, check_vma=False)
```
